32 devices in a mesh: parts: 2 (over y), expert: 16 (over z, x, core), dp: 1.
Axes of the slice: x: 2, y: 2, z: 4, core: 2. Of those that a mesh axis runs over, the one named last changes fastest.
Arguments:
- tokens: bfloat16 [2048, 2048], P(('parts', 'expert', 'dp')), parts along dimension 0, may hold values from -6 to 6
- expert_ids: int32 [2048, 8], P(('parts', 'expert', 'dp')), parts along dimension 0, may hold values from 0 to 15, all different within a row; in each aligned block of 64 rows (0 to 63, 64 to 127, ...) at most 64 rows name the same one
- router_weights: float32 [2048, 8], P(('parts', 'expert', 'dp')), parts along dimension 0, may hold values from 0.1 to 1
- w_gate: bfloat16 [16, 2048, 768], P('expert', None, 'dp'), may hold values from -0.125 to 0.125
- w_up: bfloat16 [16, 2048, 768], P('expert', None, 'dp'), may hold values from -0.125 to 0.125
- w_down: bfloat16 [16, 2048, 768], P('expert', None, 'dp'), may hold values from -0.21875 to 0.21875
Outputs:
- mixed: bfloat16 [2048, 2048], P(('parts', 'expert', 'dp')), parts along dimension 0
The draws below stay inside these ranges and needn't reach their ends.
There are 2 independent parts, one for each index of `parts`. The reference program is written for one: setup_inputs(seed, part) draws one part's arguments, and reference() takes and returns one part's arrays. A program takes and returns all parts, laid end to end along the dimension named above; an argument that names none is the same for every part. Nothing has to cross between parts.
Inputs may be any that keep to these rules, and one draw needn't show every extreme that they name: `expert_ids`: each token names 8 different experts. Among the 64 tokens of one device no expert is named more than 64 times, and in every draw some expert is named exactly 64 times by the tokens of some device.
All inputs are finite; a program needn't handle non-finite values.
Results may differ from the reference program's by a relative error of at most 0.008.
Values may be sent and summed in bfloat16 or wider, within the bound.
A program may use at most 128 MiB of HBM per device.

```python
import math
import jax
import jax.numpy as jnp
import numpy as np
from jax import lax

D = 2048
FF = 768
TOP = 8
TOK_DEV = 64
EXPERTS = 16
TOKENS = 1024
CAP = 64
N_EXPERT = 16
N_DP = 1


def block_scale(key, dims, shards, low, high):
    factor_of, own = 1.0, jax.random.fold_in(key, 6)
    for position, shards_of in shards:
        draws = jnp.exp(jax.random.uniform(jax.random.fold_in(own, position), (shards_of,), jnp.float32, low / len(shards), high / len(shards)))
        factor_of = factor_of * jnp.repeat(draws, dims[position] // shards_of).reshape([-1 if axis == position else 1 for axis in range(len(dims))])
    return factor_of


def deal_out(rng, own, number, rows, number_of, top, limit, skew):
    order = jax.random.permutation(rng, number_of)
    packed, ordinary = portions_of(number_of, rows * top, limit, skew, True), portions_of(number_of, rows * top, limit, skew, False)
    places = jnp.arange(number_of)

    def named(sizes, turn):
        used = int((sizes > 0).sum())
        fixed = max(1, used // 4)
        shifted = fixed + (places - fixed + turn * (used - fixed)) % max(1, number_of - fixed)
        return jnp.zeros((number_of,), jnp.int32).at[order[jnp.where(places < fixed, places, shifted)]].set(jnp.asarray(sizes, jnp.int32))

    sizes = jnp.where(number % 4 == 0, named(packed, number // 4), named(ordinary, number - number // 4 - 1))
    mixed = jax.random.permutation(jax.random.fold_in(own, 3), number_of)
    source_of, sink = mixed[0:number_of // 2 * 2:2], mixed[1:number_of // 2 * 2:2]
    room = jnp.minimum(sizes[source_of] - 1, limit - sizes[sink]) // 2
    room = jnp.where((source_of == order[0]) | (sink == order[0]) | (sizes[sink] == 0), 0, jnp.maximum(room, 0))
    shifted = jax.random.randint(jax.random.fold_in(own, 4), (number_of // 2,), 0, 1 << 20) % (room + 1)
    sizes = sizes.at[source_of].add(-shifted).at[sink].add(shifted)
    items = jnp.searchsorted(jnp.cumsum(sizes), jnp.arange(rows * top), side="right").astype(jnp.int32)
    grid = items.reshape(top, rows).T
    grid = grid[jax.random.permutation(jax.random.fold_in(own, 1), rows)]
    turn = jax.random.randint(jax.random.fold_in(own, 2), (rows, 1), 0, top)
    return jnp.take_along_axis(grid, (jnp.arange(top)[None, :] + turn) % top, axis=1)


def portions_of(number_of, total, bound, slope, full):
    portions = [(1 << 20) // math.isqrt(rank ** slope) + 1 for rank in range(1, number_of + 1)]
    largest = bound if full else min(bound, max(-(-total // number_of), total * portions[0] // sum(portions)))
    least = 1 if total - largest >= number_of - 1 else 0
    counts, surplus = [largest] + [least] * (number_of - 1), total - largest - least * (number_of - 1)
    while surplus > 0:
        free = [i for i in range(1, number_of) if counts[i] < largest] or [i for i in range(1, number_of) if counts[i] < bound]
        mass, remaining = sum([portions[i] for i in free]), surplus
        for i in free:
            more = min(bound - counts[i], max(1, remaining * portions[i] // mass), surplus)
            counts[i] = counts[i] + more
            surplus = surplus - more
    return np.array(counts)


def noise(stream_key, shape, scale, reach, cuts=(), kind=jnp.bfloat16):
    gain = block_scale(stream_key, shape, cuts, -0.22, 0.18) if cuts else 1.0
    values = jax.random.normal(stream_key, shape, jnp.float32) * scale * gain
    return jnp.minimum(jnp.maximum(values, -reach), reach).astype(kind)


def setup_inputs(seed: int = 0, part: int = 0) -> dict:
    streams_of = jax.random.split(jax.random.key(seed), 7)
    own_keys = jax.random.split(jax.random.fold_in(streams_of[6], part), 7)
    tokens = noise(own_keys[0], (TOKENS, D), 1.0, 6.0, ((0, 16),))
    expert_ids_keys = jax.random.split(jax.random.fold_in(own_keys[1], 1), TOKENS // TOK_DEV)
    expert_ids_turns = jax.random.permutation(jax.random.fold_in(own_keys[1], 3), TOKENS // TOK_DEV)
    expert_ids = jax.vmap(lambda own, number: deal_out(jax.random.fold_in(own_keys[1], 2), own, number, TOK_DEV, EXPERTS, TOP, CAP, 2))(expert_ids_keys, expert_ids_turns).reshape((TOKENS, TOP))
    router_weights = jnp.clip(jnp.exp(math.log(1.0) - 2.3025851 * jax.random.uniform(own_keys[2], (TOKENS, TOP), jnp.float32) ** block_scale(own_keys[2], (TOKENS, TOP), ((0, 16),), -0.2, 0.2)), 0.1, 1.0)
    w_gate = noise(streams_of[3], (EXPERTS, D, FF), D ** -0.5, 0.125, ((0, 16),))
    w_up = noise(streams_of[4], (EXPERTS, D, FF), D ** -0.5, 0.125, ((0, 16),))
    w_down = noise(streams_of[5], (EXPERTS, D, FF), FF ** -0.5, 0.21875, ((0, 16),))
    return {"tokens": tokens, "expert_ids": expert_ids, "router_weights": router_weights, "w_gate": w_gate, "w_up": w_up, "w_down": w_down}


def reference(tokens, expert_ids, router_weights, w_gate, w_up, w_down):
    maxrows = CAP * N_EXPERT * N_DP
    block = math.gcd(maxrows, 128)
    padded = jnp.concatenate([tokens, jnp.zeros((1, D), jnp.bfloat16)], 0)

    def step(accum, inputs):
        expert, gate_w, up_w, down_w = inputs
        chosen = expert_ids == expert
        weight = jnp.sum(jnp.where(chosen, router_weights, jnp.zeros_like(router_weights)), 1)
        member = jnp.any(chosen, 1)
        count = jnp.sum(member.astype(jnp.int32))
        where_rows = jnp.nonzero(member, size=maxrows, fill_value=TOKENS)[0].astype(jnp.int32)
        rows = padded[where_rows]

        def run(block_rows):
            gate_val = jnp.dot(block_rows, gate_w, preferred_element_type=jnp.float32)
            up_val = jnp.dot(block_rows, up_w, preferred_element_type=jnp.float32)
            hidden = (jax.nn.silu(gate_val) * up_val).astype(jnp.bfloat16)
            return jnp.dot(hidden, down_w.T, preferred_element_type=jnp.float32)

        def empty(block_rows):
            return jnp.zeros((block_rows.shape[0], D), jnp.float32)

        pieces = []
        for index in range(maxrows // block):
            block_rows = rows[index * block:(index + 1) * block]
            pieces.append(lax.cond(index * block < count, run, empty, block_rows))
        expert_out = lax.optimization_barrier(jnp.concatenate(pieces, 0).astype(jnp.bfloat16))
        weights_pad = jnp.concatenate([weight, jnp.zeros((1,), weight.dtype)], 0)[where_rows]
        accum = accum.at[where_rows].add(weights_pad[:, None] * expert_out.astype(jnp.float32))
        return accum, None

    start = jnp.zeros((TOKENS + 1, D), jnp.float32)
    total, unused = lax.scan(step, start, (jnp.arange(EXPERTS, dtype=jnp.int32), w_gate, w_up, w_down))
    return total[:TOKENS].astype(jnp.bfloat16)
```

```python
import functools
import math

import jax
import jax.numpy as jnp
from jax import lax
from jax.experimental import pallas as pl
from jax.experimental.pallas import tpu as pltpu
from jax.sharding import PartitionSpec as P

LANES = 128
PARTS = 3


def expert_rows(rows, gate_w, up_w, down_w):
    total = rows.shape[0]
    block = math.gcd(total, 128)
    pieces = []
    for index in range(total // block):
        block_rows = rows[index * block : (index + 1) * block]
        gate_val = jnp.dot(block_rows, gate_w, preferred_element_type=jnp.float32)
        up_val = jnp.dot(block_rows, up_w, preferred_element_type=jnp.float32)
        hidden = (jax.nn.silu(gate_val) * up_val).astype(jnp.bfloat16)
        pieces.append(
            lax.dot_general(
                hidden, down_w, (((1,), (1,)), ((), ())), preferred_element_type=jnp.float32
            )
        )
    return jnp.concatenate(pieces, 0)


def routed_body(cap, tokens, expert_ids, router_weights, w_gate, w_up, w_down):
    tok_count, top = expert_ids.shape
    width = tokens.shape[1]
    experts = lax.axis_size("expert")
    slots_all = experts * cap
    flat_ids = expert_ids.reshape(-1)
    onehot = (flat_ids[:, None] == jnp.arange(experts, dtype=jnp.int32)[None, :]).astype(jnp.int32)
    order = jnp.arange(flat_ids.shape[0], dtype=jnp.int32)
    earlier = (order[None, :] < order[:, None]).astype(jnp.bfloat16)
    before = jnp.dot(earlier, onehot.astype(jnp.bfloat16), preferred_element_type=jnp.float32).astype(jnp.int32)
    position = jnp.sum(before * onehot, 1)
    slot = flat_ids * cap + position
    send = jnp.zeros((slots_all, width), jnp.bfloat16).at[slot].set(jnp.repeat(tokens, top, 0))
    send = send.reshape(experts, cap, width)
    arrived = lax.all_to_all(send, "expert", split_axis=0, concat_axis=0, tiled=True)
    packed = arrived.reshape(slots_all, width)
    result = expert_rows(
        packed,
        lax.all_gather(w_gate, "dp", axis=2, tiled=True)[0],
        lax.all_gather(w_up, "dp", axis=2, tiled=True)[0],
        lax.all_gather(w_down, "dp", axis=2, tiled=True)[0],
    )
    expert_out = result.astype(jnp.bfloat16)
    back = lax.all_to_all(
        expert_out.reshape(experts, cap, width), "expert", split_axis=0, concat_axis=0, tiled=True
    )
    picked = back.reshape(slots_all, width)[slot].reshape(tok_count, top, width)
    mixed = jnp.einsum("tk,tkd->td", router_weights, picked.astype(jnp.float32))
    return mixed.astype(jnp.bfloat16)


def dense_body(tokens, expert_ids, router_weights, w_gate, w_up, w_down):
    experts = lax.axis_size("expert")
    axes = ("expert", "dp") if lax.axis_size("dp") > 1 else "expert"
    chosen = expert_ids[:, :, None] == jnp.arange(experts, dtype=jnp.int32)[None, None, :]
    table = jnp.sum(jnp.where(chosen, router_weights[:, :, None], 0.0), 1)
    table = lax.all_gather(table, axes, axis=0, tiled=True)
    rows = lax.all_gather(tokens, axes, axis=0, tiled=True)
    mine = jnp.arange(experts, dtype=jnp.int32)[None, :] == lax.axis_index("expert")
    weight = jnp.sum(jnp.where(mine, table, 0.0), 1, keepdims=True)
    gate_val = jnp.dot(rows, w_gate[0], preferred_element_type=jnp.float32)
    up_val = jnp.dot(rows, w_up[0], preferred_element_type=jnp.float32)
    hidden = (jax.nn.silu(gate_val) * up_val).astype(jnp.bfloat16)
    out = lax.dot_general(
        hidden, w_down[0], (((1,), (1,)), ((), ())), preferred_element_type=jnp.float32
    )
    part = (out * weight).astype(jnp.bfloat16)
    return lax.psum_scatter(part, axes, scatter_dimension=0, tiled=True)


MESH = pl.DeviceIdType.MESH
ROWS = 4
HALVES = 2
CHUNKS = 2
BLOCK = 512

EDGE = (
    ("W", 0, 0, 0), ("X", 0, 0), ("W", 0, 0, 1), ("X", 0, 1), ("Z", 0, 0, 0, 1), ("Z", 0, 0, 1, 1), ("W", 0, 1, 0),
    ("W", 1, 0, 0), ("X", 1, 0), ("GU", 0, 0), ("DN", 0, 0, 0), ("W", 0, 1, 1), ("Z", 0, 1, 1, 1), ("DN", 0, 0, 1),
    ("RX", 0, 0, 0), ("GU", 0, 1), ("W", 1, 1, 0), ("W", 2, 0, 0), ("X", 2, 0), ("RX", 0, 0, 1), ("DN", 0, 1, 0),
    ("DN", 0, 1, 1), ("GU", 1, 0), ("W", 1, 0, 1), ("RX", 0, 1, 0), ("W", 1, 1, 1), ("DN", 1, 0, 0), ("DN", 1, 0, 1),
    ("GU", 1, 1), ("W", 3, 0, 0), ("X", 3, 0), ("W", 2, 1, 0), ("DN", 1, 1, 0), ("RX", 1, 0, 0), ("DN", 1, 1, 1),
    ("GU", 2, 0), ("RX", 1, 0, 1), ("DN", 2, 0, 0), ("W", 2, 1, 1), ("DN", 2, 0, 1), ("W", 3, 1, 0), ("RX", 2, 0, 1),
    ("RX", 2, 0, 0), ("FS", 1, 0, 0), ("W", 3, 0, 1), ("RX", 1, 1, 0), ("GU", 3, 0), ("DN", 3, 0, 0),
    ("FS", 1, 0, 1), ("FS", 2, 0, 1), ("W", 3, 1, 1), ("DN", 3, 0, 1), ("RX", 3, 0, 0), ("RX", 0, 1, 1),
    ("FS", 2, 0, 0), ("GU", 3, 1), ("DN", 3, 1, 0), ("W", 2, 0, 1), ("FS", 1, 1, 0), ("RX", 3, 0, 1),
    ("DN", 3, 1, 1), ("FS", 3, 0, 0), ("RX", 3, 1, 0), ("GU", 2, 1), ("RX", 3, 1, 1), ("DN", 2, 1, 0),
    ("FS", 3, 0, 1), ("DN", 2, 1, 1), ("RX", 2, 1, 0), ("FS", 3, 1, 0), ("RX", 2, 1, 1), ("FS", 3, 1, 1),
    ("RX", 1, 1, 1), ("FS", 2, 1, 0), ("FS", 2, 1, 1), ("FS", 1, 1, 1), ("FS", 0, 1, 0), ("FS", 0, 0, 1),
    ("FS", 0, 0, 0), ("FS", 0, 1, 1),
)
INNER = (
    ("W", 1, 0, 0), ("Z", 1, 0, 0, 0), ("X", 1, 0), ("Z", 1, 0, 0, 2), ("W", 1, 0, 1), ("Z", 1, 0, 1, 0),
    ("X", 1, 1), ("Z", 1, 0, 1, 2), ("W", 2, 0, 0), ("W", 0, 0, 0), ("Z", 0, 0, 0, 2), ("X", 0, 0), ("W", 1, 1, 0),
    ("Z", 2, 0, 0, 0), ("X", 2, 0), ("GU", 1, 0), ("W", 1, 1, 1), ("Z", 1, 1, 1, 0), ("W", 0, 0, 1), ("DN", 1, 0, 0),
    ("Z", 1, 1, 1, 2), ("DN", 1, 0, 1), ("GU", 1, 1), ("W", 0, 1, 0), ("DN", 1, 1, 0), ("W", 3, 0, 0),
    ("Z", 3, 0, 0, 0), ("Z", 0, 0, 1, 2), ("DN", 1, 1, 1), ("GU", 0, 0), ("W", 0, 1, 1), ("DN", 0, 0, 0),
    ("W", 2, 1, 0), ("DN", 0, 0, 1), ("W", 2, 1, 1), ("RX", 1, 1, 1), ("Z", 0, 1, 1, 2), ("W", 2, 0, 1), ("X", 3, 0),
    ("Z", 2, 1, 1, 0), ("GU", 0, 1), ("DN", 0, 1, 0), ("W", 3, 0, 1), ("RX", 0, 0, 1), ("Z", 3, 0, 1, 0),
    ("RX", 0, 0, 0), ("DN", 0, 1, 1), ("GU", 2, 0), ("W", 3, 1, 1), ("DN", 2, 0, 0), ("Z", 3, 1, 1, 0),
    ("DN", 2, 0, 1), ("GU", 2, 1), ("RX", 2, 0, 1), ("W", 3, 1, 0), ("RX", 0, 1, 0), ("Z", 2, 0, 1, 0),
    ("DN", 2, 1, 0), ("DN", 2, 1, 1), ("RX", 1, 1, 0), ("GU", 3, 0), ("DN", 3, 0, 0), ("RX", 1, 0, 1),
    ("DN", 3, 0, 1), ("RX", 2, 0, 0), ("RX", 3, 0, 0), ("GU", 3, 1), ("RX", 3, 0, 1), ("RX", 2, 1, 0),
    ("DN", 3, 1, 0), ("FS", 2, 0, 1), ("DN", 3, 1, 1), ("RX", 3, 1, 0), ("RX", 3, 1, 1), ("FS", 2, 0, 0),
    ("RX", 2, 1, 1), ("FS", 3, 0, 0), ("FS", 3, 0, 1), ("RX", 0, 1, 1), ("FS", 3, 1, 0), ("FS", 0, 0, 0),
    ("FS", 3, 1, 1), ("FS", 0, 0, 1), ("RX", 1, 0, 0), ("FS", 2, 1, 0), ("FS", 0, 1, 0), ("FS", 1, 0, 1),
    ("FS", 2, 1, 1), ("FS", 0, 1, 1), ("FS", 1, 1, 0), ("FS", 1, 0, 0), ("FS", 1, 1, 1),
)


def friendly(number):
    sizes = []
    while number:
        size = max(v for v in (16, 12, 8, 6, 4, 3, 2, 1) if v <= number)
        sizes.append(size)
        number -= size
    return sizes


def fused_kernel(
    token_ref, table_ref, gate_hbm, up_hbm, down_hbm, out_ref,
    tok, gate_w, up_w, down_w, hid, part, from_core, to_x, from_x, to_z, from_z,
    load_sem, own_sem, ag_recv, agc_recv, rsc_recv, rsx_recv, rsz_recv, agz_send, agx_send, other_send,
):
    me = lax.axis_index("expert")
    core = lax.rem(me, 2)
    col = lax.rem(me // 2, 2)
    row = me // 4
    width = out_ref.shape[1]
    half = tok.shape[4]
    cols = width // CHUNKS
    flip = row // 2
    edge = (row == 0) | (row == ROWS - 1)
    slab = [s + flip * (ROWS - 1 - 2 * s) for s in range(ROWS)]

    def device(r, x, c):
        return {"expert": (r * 2 + x) * 2 + c}

    partner = device(row, col, 1 - core)
    beside = device(row, 1 - col, core)
    above = device(row + 1, col, core)
    below = device(row - 1, col, core)

    loads = [
        pltpu.make_async_copy(gate_hbm.at[0], gate_w, load_sem.at[0]),
        pltpu.make_async_copy(up_hbm.at[0], up_w, load_sem.at[1]),
        pltpu.make_async_copy(down_hbm.at[0], down_w, load_sem.at[2]),
    ]
    owns = [
        pltpu.make_async_copy(token_ref, tok.at[row, core, col, :, :, pl.ds(0, width)], own_sem.at[0]),
        pltpu.make_async_copy(table_ref, tok.at[row, core, col, :, :, pl.ds(width, LANES)], own_sem.at[1]),
    ]

    barrier = pltpu.get_barrier_semaphore()
    for other in (partner, beside):
        pl.semaphore_signal(barrier, inc=1, device_id=other, device_id_type=MESH)

    @pl.when(row > 0)
    def _():
        pl.semaphore_signal(barrier, inc=1, device_id=below, device_id_type=MESH)

    @pl.when(row < ROWS - 1)
    def _():
        pl.semaphore_signal(barrier, inc=1, device_id=above, device_id_type=MESH)

    for own in owns:
        own.start()
    for load in loads:
        load.start()
    pl.semaphore_wait(barrier, jnp.where(edge, 3, 4))
    for own in owns:
        own.wait()

    def remote(src, dst, send_sem, recv_sem, target):
        return pltpu.make_async_remote_copy(
            src_ref=src, dst_ref=dst, send_sem=send_sem, recv_sem=recv_sem,
            device_id=target, device_id_type=MESH,
        )

    def column(x):
        return 1 - col if x else col

    def token_copy(s, x, h, send_sem, target):
        block = tok.at[slab[s], core, column(x), h]
        return remote(block, block, send_sem, ag_recv.at[slab[s], column(x), h], target)

    def token_core(s, x, h, mine):
        block = tok.at[s, core if mine else 1 - core, x, h]
        return remote(block, block, other_send.at[0], agc_recv.at[s, x, h], partner)

    def part_core(s, h, q):
        return remote(
            part.at[s, h, q, 1 - core], from_core.at[s, h, q], other_send.at[1], rsc_recv.at[s, h, q], partner
        )

    def sum_x(s, h, q):
        return remote(to_x.at[s, h, q], from_x.at[s, h, q], other_send.at[2], rsx_recv.at[s, h, q], beside)

    def sum_z(s, h, q, way, target):
        return remote(
            to_z.at[s, h, q], from_z.at[way, s, h, q], other_send.at[3], rsz_recv.at[way, s, h, q], target
        )

    def core_sum(s, h, q, x):
        mine = part[s, h, q, core, x].astype(jnp.float32)
        return mine + from_core[s, h, q, x].astype(jnp.float32)

    class Line:
        def __init__(self, near, program):
            self.near = near
            self.program = program
            counts = {"Z": 0, "X": 0}
            for act in program:
                if act[0] in counts:
                    counts[act[0]] += 1
            self.sems = {}
            self.sizes = {}
            for name, sem in (("Z", agz_send), ("X", agx_send)):
                self.sizes[name] = friendly(counts[name])
                self.sems[name] = [
                    sem.at[at] for at, size in enumerate(self.sizes[name]) for _ in range(size)
                ]
            self.slots = [[]]
            for act in program:
                if act[0] in ("GU", "DN"):
                    self.slots.append([])
                else:
                    self.slots[-1].append(act)
            self.order = [act[1:] for act in program if act[0] == "GU"]

        def toward(self, n):
            return device(slab[n], col, core)

        def run(self, at):
            for act in self.slots[at]:
                getattr(self, act[0])(*act[1:])

        def W(self, s, x, h):
            if not (s == self.near and x == 0):
                token_copy(s, x, h, agz_send.at[0], beside).wait_recv()
            token_core(slab[s], column(x), h, True).start()

        def Z(self, s, x, h, n):
            token_copy(s, x, h, self.sems["Z"].pop(), self.toward(n)).start()

        def X(self, s, h):
            token_copy(s, 0, h, self.sems["X"].pop(), beside).start()

        def RX(self, s, h, q):
            s = slab[s]
            part_core(s, h, q).wait_recv()
            to_x[s, h, q] = core_sum(s, h, q, 1 - col).astype(jnp.bfloat16)
            sum_x(s, h, q).start()

        def FS(self, s, h, q):
            far = abs(self.near - s)
            at = slab[s]
            sum_x(at, h, q).wait_recv()
            total = core_sum(at, h, q, col) + from_x[at, h, q].astype(jnp.float32)
            for n in (self.near - 1, self.near + 1):
                if 0 <= n < ROWS and abs(n - s) > far:
                    way = flip if n < self.near else 1 - flip
                    sum_z(at, h, q, way, beside).wait_recv()
                    total = total + from_z[way, at, h, q].astype(jnp.float32)
            total = total.astype(jnp.bfloat16)
            if far == 0:
                out_ref[h * half : (h + 1) * half, q * cols : (q + 1) * cols] = total
            else:
                to_z[at, h, q] = total
                n = self.near - 1 if s < self.near else self.near + 1
                way = flip if n > self.near else 1 - flip
                sum_z(at, h, q, way, self.toward(n)).start()

        def sent(self):
            for name, sem in (("Z", agz_send), ("X", agx_send)):
                for at, size in enumerate(self.sizes[name]):
                    lead = size // 4 if size % 4 == 0 else size // 2 if size % 2 == 0 else size
                    inner = size // lead
                    block = tok.at[pl.ds(0, lead), pl.ds(0, 1), pl.ds(0, max(1, inner // 2)), pl.ds(0, min(2, inner))]
                    pltpu.make_async_copy(block, block, sem.at[at]).wait()

    lines = [(edge, Line(0, EDGE)), (jnp.logical_not(edge), Line(1, INNER))]

    def hook(at):
        for here, line in lines:
            if line.slots[at]:
                pl.when(here)(functools.partial(line.run, at))

    lane = lax.broadcasted_iota(jnp.int32, (1, LANES), 1)
    pick = jnp.where((lane % (ROWS * 4) == me) & (lane < PARTS * ROWS * 4), 1.0, 0.0)

    def place(k):
        (s0, h0), (s1, h1) = lines[0][1].order[k], lines[1][1].order[k]
        s = slab[s0] if s0 == s1 else jnp.where(edge, slab[s0], slab[s1])
        h = h0 if h0 == h1 else jnp.where(edge, h0, h1)
        return s, h

    at = 0
    for k in range(ROWS * HALVES):
        hook(at)
        s, h = place(k)
        for x in range(2):
            token_core(s, x, h, False).wait_recv()
        if k == 0:
            loads[0].wait()
            loads[1].wait()
        rows = tok[s, :, :, h].reshape(4 * half, width + LANES)
        weight = jnp.sum(rows[:, width:].astype(jnp.float32) * pick, 1, keepdims=True)
        rows = rows[:, :width]
        gate_val = jnp.dot(rows, gate_w[...], preferred_element_type=jnp.float32)
        up_val = jnp.dot(rows, up_w[...], preferred_element_type=jnp.float32)
        hid[...] = (gate_val / (1.0 + jnp.exp(-gate_val)) * up_val).astype(jnp.bfloat16)
        at += 1
        if k == 0:
            loads[2].wait()
        for q in range(CHUNKS):
            hook(at)
            for b in range(0, cols, BLOCK):
                value = lax.dot_general(
                    hid[...], down_w[q * cols + b : q * cols + b + BLOCK, :], (((1,), (1,)), ((), ())),
                    preferred_element_type=jnp.float32,
                )
                part[s, h, q, :, :, :, b : b + BLOCK] = (
                    (value * weight).astype(jnp.bfloat16).reshape(2, 2, half, BLOCK)
                )
            part_core(s, h, q).start()
            at += 1
    hook(at)

    for here, line in lines:
        pl.when(here)(line.sent)
    both = tok.at[pl.ds(0, 2)]
    pltpu.make_async_copy(both, both, other_send.at[0]).wait()
    pltpu.make_async_copy(from_core, from_core, other_send.at[1]).wait()
    pltpu.make_async_copy(to_x, to_x, other_send.at[2]).wait()
    most = to_z.at[pl.ds(0, ROWS - 1)]
    pltpu.make_async_copy(most, most, other_send.at[3]).wait()


def fused_body(tokens, expert_ids, router_weights, w_gate, w_up, w_down):
    experts = lax.axis_size("expert")
    count, width = tokens.shape
    ff = w_gate.shape[2]
    half = count // HALVES
    chosen = expert_ids[:, :, None] == jnp.arange(experts, dtype=jnp.int32)[None, None, :]
    left = jnp.sum(jnp.where(chosen, router_weights[:, :, None], 0.0), 1)
    terms = []
    for _ in range(PARTS):
        term = lax.reduce_precision(left, 8, 7)
        left = left - term
        terms.append(term.astype(jnp.bfloat16))
    pad = jnp.zeros((count, LANES - PARTS * experts), jnp.bfloat16)
    table = jnp.concatenate(terms + [pad], 1).reshape(HALVES, half, LANES)
    wide = width + LANES
    cols = width // CHUNKS
    bf16 = jnp.bfloat16
    dma = pltpu.SemaphoreType.DMA
    each = (ROWS, HALVES, CHUNKS)
    return pl.pallas_call(
        fused_kernel,
        out_shape=jax.ShapeDtypeStruct((count, width), bf16),
        in_specs=[pl.BlockSpec(memory_space=pl.ANY)] * 5,
        out_specs=pl.BlockSpec(memory_space=pltpu.VMEM),
        scratch_shapes=[
            pltpu.VMEM((ROWS, 2, 2, HALVES, half, wide), bf16),
            pltpu.VMEM((width, ff), bf16),
            pltpu.VMEM((width, ff), bf16),
            pltpu.VMEM((width, ff), bf16),
            pltpu.VMEM((4 * half, ff), bf16),
            pltpu.VMEM(each + (2, 2, half, cols), bf16),
            pltpu.VMEM(each + (2, half, cols), bf16),
            pltpu.VMEM(each + (half, cols), bf16),
            pltpu.VMEM(each + (half, cols), bf16),
            pltpu.VMEM(each + (half, cols), bf16),
            pltpu.VMEM((2,) + each + (half, cols), bf16),
            dma((3,)), dma((2,)), dma((ROWS, 2, HALVES)), dma((ROWS, 2, HALVES)), dma(each), dma(each), dma((2,) + each),
            dma((4,)), dma((4,)), dma((4,)),
        ],
        compiler_params=pltpu.CompilerParams(
            collective_id=0, has_side_effects=True, vmem_limit_bytes=60 * 1024 * 1024
        ),
        name="moe",
    )(tokens.reshape(HALVES, half, width), table, w_gate, w_up, w_down)


def body(tokens, expert_ids, router_weights, w_gate, w_up, w_down):
    tok_count, top = expert_ids.shape
    experts = lax.axis_size("expert")
    cap = max(2, min(tok_count, 2 * tok_count * top // experts))
    args = (tokens, expert_ids, router_weights, w_gate, w_up, w_down)
    grid = experts == 4 * ROWS and lax.axis_size("dp") == 1 and tok_count % (16 * HALVES) == 0
    if cap >= tok_count and grid:
        return fused_body(*args)
    if cap >= tok_count:
        return dense_body(*args)
    return routed_body(cap, *args)


def solution(mesh):
    in_specs = (
        P(("parts", "expert", "dp"), None),
        P(("parts", "expert", "dp"), None),
        P(("parts", "expert", "dp"), None),
        P("expert", None, "dp"),
        P("expert", None, "dp"),
        P("expert", None, "dp"),
    )
    out_specs = P(("parts", "expert", "dp"), None)
    return jax.shard_map(body, mesh=mesh, in_specs=in_specs, out_specs=out_specs, check_vma=False)
```

```python
import functools
import math

import jax
import jax.numpy as jnp
from jax import lax
from jax.experimental import pallas as pl
from jax.experimental.pallas import tpu as pltpu
from jax.sharding import PartitionSpec as P

LANES = 128
PARTS = 3


def expert_rows(rows, gate_w, up_w, down_w):
    total = rows.shape[0]
    block = math.gcd(total, 128)
    pieces = []
    for index in range(total // block):
        block_rows = rows[index * block : (index + 1) * block]
        gate_val = jnp.dot(block_rows, gate_w, preferred_element_type=jnp.float32)
        up_val = jnp.dot(block_rows, up_w, preferred_element_type=jnp.float32)
        hidden = (jax.nn.silu(gate_val) * up_val).astype(jnp.bfloat16)
        pieces.append(
            lax.dot_general(
                hidden, down_w, (((1,), (1,)), ((), ())), preferred_element_type=jnp.float32
            )
        )
    return jnp.concatenate(pieces, 0)


def routed_body(cap, tokens, expert_ids, router_weights, w_gate, w_up, w_down):
    tok_count, top = expert_ids.shape
    width = tokens.shape[1]
    experts = lax.axis_size("expert")
    slots_all = experts * cap
    flat_ids = expert_ids.reshape(-1)
    onehot = (flat_ids[:, None] == jnp.arange(experts, dtype=jnp.int32)[None, :]).astype(jnp.int32)
    order = jnp.arange(flat_ids.shape[0], dtype=jnp.int32)
    earlier = (order[None, :] < order[:, None]).astype(jnp.bfloat16)
    before = jnp.dot(earlier, onehot.astype(jnp.bfloat16), preferred_element_type=jnp.float32).astype(jnp.int32)
    position = jnp.sum(before * onehot, 1)
    slot = flat_ids * cap + position
    send = jnp.zeros((slots_all, width), jnp.bfloat16).at[slot].set(jnp.repeat(tokens, top, 0))
    send = send.reshape(experts, cap, width)
    arrived = lax.all_to_all(send, "expert", split_axis=0, concat_axis=0, tiled=True)
    packed = arrived.reshape(slots_all, width)
    result = expert_rows(
        packed,
        lax.all_gather(w_gate, "dp", axis=2, tiled=True)[0],
        lax.all_gather(w_up, "dp", axis=2, tiled=True)[0],
        lax.all_gather(w_down, "dp", axis=2, tiled=True)[0],
    )
    expert_out = result.astype(jnp.bfloat16)
    back = lax.all_to_all(
        expert_out.reshape(experts, cap, width), "expert", split_axis=0, concat_axis=0, tiled=True
    )
    picked = back.reshape(slots_all, width)[slot].reshape(tok_count, top, width)
    mixed = jnp.einsum("tk,tkd->td", router_weights, picked.astype(jnp.float32))
    return mixed.astype(jnp.bfloat16)


def dense_body(tokens, expert_ids, router_weights, w_gate, w_up, w_down):
    experts = lax.axis_size("expert")
    axes = ("expert", "dp") if lax.axis_size("dp") > 1 else "expert"
    chosen = expert_ids[:, :, None] == jnp.arange(experts, dtype=jnp.int32)[None, None, :]
    table = jnp.sum(jnp.where(chosen, router_weights[:, :, None], 0.0), 1)
    table = lax.all_gather(table, axes, axis=0, tiled=True)
    rows = lax.all_gather(tokens, axes, axis=0, tiled=True)
    mine = jnp.arange(experts, dtype=jnp.int32)[None, :] == lax.axis_index("expert")
    weight = jnp.sum(jnp.where(mine, table, 0.0), 1, keepdims=True)
    gate_val = jnp.dot(rows, w_gate[0], preferred_element_type=jnp.float32)
    up_val = jnp.dot(rows, w_up[0], preferred_element_type=jnp.float32)
    hidden = (jax.nn.silu(gate_val) * up_val).astype(jnp.bfloat16)
    out = lax.dot_general(
        hidden, w_down[0], (((1,), (1,)), ((), ())), preferred_element_type=jnp.float32
    )
    part = (out * weight).astype(jnp.bfloat16)
    return lax.psum_scatter(part, axes, scatter_dimension=0, tiled=True)


MESH = pl.DeviceIdType.MESH
ROWS = 4
HALVES = 2
CHUNKS = 2
BLOCK = 512

EDGE = (
    ("W", 0, 0, 0), ("X", 0, 0), ("Z", 0, 0, 0, 1), ("W", 0, 0, 1), ("X", 0, 1), ("W", 1, 0, 0), ("Z", 0, 0, 1, 1),
    ("X", 1, 0), ("W", 0, 1, 0), ("GU", 0, 0), ("W", 0, 1, 1), ("W", 1, 0, 1), ("Z", 0, 1, 1, 1), ("DN", 0, 0, 0),
    ("DN", 0, 0, 1), ("GU", 0, 1), ("W", 1, 1, 0), ("RX", 0, 0, 1), ("W", 2, 0, 0), ("DN", 0, 1, 0), ("X", 2, 0),
    ("DN", 0, 1, 1), ("GU", 1, 0), ("DN", 1, 0, 0), ("W", 1, 1, 1), ("DN", 1, 0, 1), ("RX", 1, 0, 0), ("GU", 1, 1),
    ("W", 3, 0, 0), ("X", 3, 0), ("RX", 1, 0, 1), ("W", 2, 1, 0), ("DN", 1, 1, 0), ("DN", 1, 1, 1), ("GU", 2, 0),
    ("FS", 1, 0, 0), ("DN", 2, 0, 0), ("DN", 2, 0, 1), ("W", 3, 1, 0), ("RX", 1, 1, 1), ("RX", 2, 0, 0),
    ("RX", 2, 0, 1), ("W", 3, 0, 1), ("GU", 3, 0), ("DN", 3, 0, 0), ("FS", 1, 0, 1), ("FS", 1, 1, 1), ("W", 3, 1, 1),
    ("W", 2, 0, 1), ("DN", 3, 0, 1), ("RX", 3, 0, 0), ("RX", 0, 1, 0), ("FS", 2, 0, 0), ("GU", 3, 1),
    ("DN", 3, 1, 0), ("W", 2, 1, 1), ("RX", 3, 0, 1), ("DN", 3, 1, 1), ("FS", 2, 0, 1), ("FS", 3, 0, 0),
    ("RX", 3, 1, 0), ("GU", 2, 1), ("DN", 2, 1, 0), ("RX", 3, 1, 1), ("FS", 3, 0, 1), ("DN", 2, 1, 1),
    ("RX", 2, 1, 0), ("FS", 3, 1, 0), ("RX", 2, 1, 1), ("RX", 1, 1, 0), ("RX", 0, 0, 0), ("RX", 0, 1, 1),
    ("FS", 3, 1, 1), ("FS", 2, 1, 0), ("FS", 2, 1, 1), ("FS", 0, 0, 1), ("FS", 1, 1, 0), ("FS", 0, 1, 0),
    ("FS", 0, 0, 0), ("FS", 0, 1, 1),
)
INNER = (
    ("W", 1, 0, 1), ("W", 1, 0, 0), ("Z", 1, 0, 0, 0), ("Z", 1, 0, 1, 0), ("Z", 1, 0, 0, 2), ("X", 1, 0),
    ("Z", 1, 0, 1, 2), ("X", 1, 1), ("W", 0, 0, 0), ("Z", 0, 0, 0, 2), ("W", 2, 0, 0), ("Z", 2, 0, 0, 0),
    ("W", 1, 1, 0), ("X", 2, 0), ("X", 0, 0), ("GU", 1, 0), ("W", 1, 1, 1), ("DN", 1, 0, 0), ("Z", 1, 1, 1, 0),
    ("DN", 1, 0, 1), ("W", 2, 0, 1), ("Z", 1, 1, 1, 2), ("GU", 1, 1), ("W", 3, 0, 0), ("W", 2, 1, 0),
    ("Z", 3, 0, 0, 0), ("DN", 1, 1, 0), ("Z", 2, 0, 1, 0), ("W", 0, 0, 1), ("RX", 1, 0, 1), ("X", 3, 0),
    ("DN", 1, 1, 1), ("Z", 0, 0, 1, 2), ("GU", 2, 0), ("DN", 2, 0, 0), ("W", 0, 1, 0), ("W", 0, 1, 1),
    ("DN", 2, 0, 1), ("RX", 2, 0, 0), ("Z", 0, 1, 1, 2), ("GU", 0, 0), ("RX", 2, 0, 1), ("W", 3, 0, 1),
    ("Z", 3, 0, 1, 0), ("DN", 0, 0, 0), ("RX", 1, 1, 0), ("DN", 0, 0, 1), ("W", 3, 1, 0), ("GU", 0, 1),
    ("FS", 2, 0, 0), ("W", 3, 1, 1), ("Z", 3, 1, 1, 0), ("W", 2, 1, 1), ("RX", 0, 0, 0), ("DN", 0, 1, 0),
    ("Z", 2, 1, 1, 0), ("FS", 2, 0, 1), ("DN", 0, 1, 1), ("RX", 0, 0, 1), ("RX", 0, 1, 0), ("GU", 3, 0),
    ("DN", 3, 0, 0), ("RX", 0, 1, 1), ("RX", 1, 1, 1), ("DN", 3, 0, 1), ("RX", 3, 0, 0), ("FS", 0, 0, 0),
    ("RX", 1, 0, 0), ("GU", 3, 1), ("DN", 3, 1, 0), ("FS", 0, 1, 0), ("DN", 3, 1, 1), ("FS", 0, 0, 1),
    ("RX", 3, 0, 1), ("GU", 2, 1), ("DN", 2, 1, 0), ("DN", 2, 1, 1), ("RX", 3, 1, 0), ("FS", 0, 1, 1),
    ("FS", 1, 0, 0), ("RX", 3, 1, 1), ("FS", 3, 0, 0), ("RX", 2, 1, 0), ("FS", 3, 0, 1), ("FS", 1, 0, 1),
    ("FS", 3, 1, 0), ("RX", 2, 1, 1), ("FS", 3, 1, 1), ("FS", 2, 1, 0), ("FS", 2, 1, 1), ("FS", 1, 1, 0),
    ("FS", 1, 1, 1),
)
DIRECT = ((0, 2, 0, 0), (0, 2, 0, 1), (1, 3, 0, 0), (1, 3, 0, 1), (1, 3, 1, 0), (1, 3, 1, 1))


def straight(n, s, h, q):
    return ((n, s, h, q) if n < ROWS // 2 else (ROWS - 1 - n, ROWS - 1 - s, h, q)) in DIRECT


def friendly(number):
    sizes = []
    while number:
        size = max(v for v in (16, 12, 8, 6, 4, 3, 2, 1) if v <= number)
        sizes.append(size)
        number -= size
    return sizes


def fused_kernel(
    token_ref, ids_hbm, scale_hbm, gate_hbm, up_hbm, down_hbm, out_hbm,
    tok, ids, scale, done, gate_w, up_w, down_w, hid, part, from_core, to_x, from_x, to_z, from_z,
    load_sem, own_sem, done_sem, ag_recv, agc_recv, rsc_recv, rsx_recv, rsz_recv, agz_send, agx_send, agc_send, other_send,
):
    me = lax.axis_index("expert")
    core = lax.rem(me, 2)
    col = lax.rem(me // 2, 2)
    row = me // 4
    width = token_ref.shape[2]
    half = tok.shape[4]
    cols = width // CHUNKS
    flip = row // 2
    edge = (row == 0) | (row == ROWS - 1)
    slab = [s + flip * (ROWS - 1 - 2 * s) for s in range(ROWS)]

    def device(r, x, c):
        return {"expert": (r * 2 + x) * 2 + c}

    partner = device(row, col, 1 - core)
    beside = device(row, 1 - col, core)

    loads = [
        pltpu.make_async_copy(gate_hbm.at[0], gate_w, load_sem.at[0]),
        pltpu.make_async_copy(up_hbm.at[0], up_w, load_sem.at[1]),
        pltpu.make_async_copy(down_hbm.at[0], down_w, load_sem.at[2]),
    ]
    owns = [
        pltpu.make_async_copy(ids_hbm, ids, own_sem.at[0]),
        pltpu.make_async_copy(scale_hbm, scale, own_sem.at[1]),
        pltpu.make_async_copy(token_ref, tok.at[row, core, col, :, :, pl.ds(0, width)], own_sem.at[2]),
    ]

    barrier = pltpu.get_barrier_semaphore()
    others = [partner, beside] + [device(lax.rem(row + n, ROWS), col, core) for n in range(1, ROWS)]
    for other in others:
        pl.semaphore_signal(barrier, inc=1, device_id=other, device_id_type=MESH)
    for own in owns:
        own.start()
    for load in loads:
        load.start()
    owns[0].wait()
    owns[1].wait()
    number = ROWS * 4
    kinds = lax.broadcasted_iota(jnp.int32, (number, 1), 0)
    left = jnp.zeros((number, HALVES * half), jnp.float32)
    for k in range(ids.shape[0]):
        left = left + jnp.where(ids[k : k + 1, :] == kinds, scale[k : k + 1, :], 0.0)
    terms = []
    for _ in range(PARTS):
        term = left.astype(jnp.bfloat16).astype(jnp.float32)
        left = left - term
        terms.append(term)
    terms = jnp.concatenate(terms, 0)
    span = LANES // HALVES
    line_at = lax.broadcasted_iota(jnp.int32, (PARTS * number, LANES), 0)
    lane_at = lax.broadcasted_iota(jnp.int32, (PARTS * number, LANES), 1)
    table = jnp.zeros((half, LANES), jnp.float32)
    for h in range(HALVES):
        move = jnp.where(lane_at == line_at + h * span, 1.0, 0.0)
        moved = lax.dot_general(terms, move, (((0,), (0,)), ((), ())), preferred_element_type=jnp.float32)
        table = table + moved[h * half : (h + 1) * half]
    tok[row, core, col, 0, :, width : width + LANES] = table.astype(jnp.bfloat16)
    pl.semaphore_wait(barrier, len(others))
    owns[2].wait()

    def remote(src, dst, send_sem, recv_sem, target):
        return pltpu.make_async_remote_copy(
            src_ref=src, dst_ref=dst, send_sem=send_sem, recv_sem=recv_sem,
            device_id=target, device_id_type=MESH,
        )

    def column(x):
        return 1 - col if x else col

    def chunk(s, c, x, h):
        return tok.at[s, c, x, h] if h == 0 else tok.at[s, c, x, h, :, pl.ds(0, width)]

    def token_copy(s, x, h, send_sem, target):
        block = chunk(slab[s], core, column(x), h)
        return remote(block, block, send_sem, ag_recv.at[slab[s], column(x), h], target)

    def token_core(s, x, h, mine):
        block = chunk(s, core if mine else 1 - core, x, h)
        return remote(block, block, agc_send.at[h], agc_recv.at[s, x, h], partner)

    def part_core(s, h, q):
        return remote(
            part.at[s, h, q, 1 - core], from_core.at[s, h, q], other_send.at[1], rsc_recv.at[s, h, q], partner
        )

    def sum_x(s, h, q):
        return remote(to_x.at[s, h, q], from_x.at[s, h, q], other_send.at[2], rsx_recv.at[s, h, q], beside)

    def sum_z(s, h, q, n, target):
        return remote(
            to_z.at[s, h, q], from_z.at[n, s, h, q], other_send.at[3], rsz_recv.at[n, s, h, q], target
        )

    def core_sum(s, h, q, x):
        mine = part[s, h, q, core, x].astype(jnp.float32)
        return mine + from_core[s, h, q, x].astype(jnp.float32)

    def batch(size, h, sem):
        lead = size // 4 if size % 4 == 0 else size // 2 if size % 2 == 0 else size
        inner = size // lead
        block = tok.at[pl.ds(0, lead), pl.ds(0, max(1, inner // 2)), pl.ds(0, min(2, inner)), h]
        if h:
            block = block.at[:, :, :, :, pl.ds(0, width)]
        return pltpu.make_async_copy(block, block, sem)

    class Line:
        def __init__(self, near, program):
            self.near = near
            self.program = program
            counts = {}
            for act in program:
                if act[0] in ("Z", "X"):
                    kind = (act[0], act[-1] if act[0] == "X" else act[3])
                    counts[kind] = counts.get(kind, 0) + 1
            self.sems = {}
            self.sizes = {}
            for kind, number in sorted(counts.items()):
                sem = agz_send if kind[0] == "Z" else agx_send
                self.sizes[kind] = friendly(number)
                self.sems[kind] = [
                    sem.at[kind[1], at] for at, size in enumerate(self.sizes[kind]) for _ in range(size)
                ]
            self.slots = [[]]
            for act in program:
                if act[0] in ("GU", "DN"):
                    self.slots.append([])
                else:
                    self.slots[-1].append(act)
            self.order = [act[1:] for act in program if act[0] == "GU"]

        def toward(self, n):
            return device(slab[n], col, core)

        def run(self, at):
            for act in self.slots[at]:
                getattr(self, act[0])(*act[1:])

        def W(self, s, x, h):
            if not (s == self.near and x == 0):
                token_copy(s, x, h, agz_send.at[0, 0], beside).wait_recv()
            token_core(slab[s], column(x), h, True).start()

        def Z(self, s, x, h, n):
            token_copy(s, x, h, self.sems["Z", h].pop(), self.toward(n)).start()

        def X(self, s, h):
            token_copy(s, 0, h, self.sems["X", h].pop(), beside).start()

        def RX(self, s, h, q):
            s = slab[s]
            part_core(s, h, q).wait_recv()
            to_x[s, h, q] = core_sum(s, h, q, 1 - col).astype(jnp.bfloat16)
            sum_x(s, h, q).start()

        def FS(self, s, h, q):
            far = abs(self.near - s)
            at = slab[s]
            sum_x(at, h, q).wait_recv()
            total = core_sum(at, h, q, col) + from_x[at, h, q].astype(jnp.float32)
            for n in range(ROWS):
                beyond = abs(n - s) > far and (far == 0 or (n < self.near) == (self.near < s))
                beside_me = abs(n - self.near) == 1 and not (far and straight(n, s, h, q))
                if beyond and (beside_me or (far == 0 and straight(n, s, h, q))):
                    sum_z(at, h, q, slab[n], beside).wait_recv()
                    total = total + from_z[slab[n], at, h, q].astype(jnp.float32)
            total = total.astype(jnp.bfloat16)
            if far == 0:
                done[h, q] = total
                self.store(h, q).start()
            else:
                to_z[at, h, q] = total
                n = self.near - 1 if s < self.near else self.near + 1
                if straight(self.near, s, h, q):
                    n = s
                sum_z(at, h, q, row, self.toward(n)).start()

        def store(self, h, q):
            place = out_hbm.at[pl.ds(h * half, half), pl.ds(q * cols, cols)]
            return pltpu.make_async_copy(done.at[h, q], place, done_sem.at[h, q])

        def sent(self):
            for (name, h), sizes in self.sizes.items():
                sem = agz_send if name == "Z" else agx_send
                for at, size in enumerate(sizes):
                    batch(size, h, sem.at[h, at]).wait()
            for h in range(HALVES):
                for q in range(CHUNKS):
                    self.store(h, q).wait()

    lines = [(edge, Line(0, EDGE)), (jnp.logical_not(edge), Line(1, INNER))]

    def hook(at):
        for here, line in lines:
            if line.slots[at]:
                pl.when(here)(functools.partial(line.run, at))

    lane = lax.broadcasted_iota(jnp.int32, (1, LANES), 1)

    def place(k):
        (s0, h0), (s1, h1) = lines[0][1].order[k], lines[1][1].order[k]
        s = slab[s0] if s0 == s1 else jnp.where(edge, slab[s0], slab[s1])
        return s, h0, h1

    at = 0
    for k in range(ROWS * HALVES):
        hook(at)
        s, h0, h1 = place(k)
        h = h0 if h0 == h1 else jnp.where(edge, h0, h1)
        if h0 == h1:
            for x in range(2):
                token_core(s, x, h0, False).wait_recv()
        else:
            for (here, _), mine in zip(lines, (h0, h1)):
                @pl.when(here)
                def _():
                    for x in range(2):
                        token_core(s, x, mine, False).wait_recv()
        pick = (lane // span == h) & (lane % span < PARTS * number) & (lane % number == me)
        tables = tok[s, :, :, 0, :, width : width + LANES].reshape(4 * half, LANES).astype(jnp.float32)
        weight = jnp.sum(jnp.where(pick, tables, 0.0), 1, keepdims=True)
        if k == 0:
            loads[0].wait()
            loads[1].wait()
        rows = tok[s, :, :, h, :, 0:width].reshape(4 * half, width)
        gate_val = jnp.dot(rows, gate_w[...], preferred_element_type=jnp.float32)
        up_val = jnp.dot(rows, up_w[...], preferred_element_type=jnp.float32)
        hid[...] = (gate_val / (1.0 + jnp.exp(-gate_val)) * up_val).astype(jnp.bfloat16)
        at += 1
        if k == 0:
            loads[2].wait()
        for q in range(CHUNKS):
            hook(at)
            for b in range(0, cols, BLOCK):
                value = lax.dot_general(
                    hid[...], down_w[q * cols + b : q * cols + b + BLOCK, :], (((1,), (1,)), ((), ())),
                    preferred_element_type=jnp.float32,
                )
                part[s, h, q, :, :, :, b : b + BLOCK] = (
                    (value * weight).astype(jnp.bfloat16).reshape(2, 2, half, BLOCK)
                )
            part_core(s, h, q).start()
            at += 1
    hook(at)

    for here, line in lines:
        pl.when(here)(line.sent)
    for h in range(HALVES):
        batch(2 * ROWS, h, agc_send.at[h]).wait()
    pltpu.make_async_copy(from_core, from_core, other_send.at[1]).wait()
    pltpu.make_async_copy(to_x, to_x, other_send.at[2]).wait()
    most = to_z.at[pl.ds(0, ROWS - 1)]
    pltpu.make_async_copy(most, most, other_send.at[3]).wait()


def fused_body(tokens, expert_ids, router_weights, w_gate, w_up, w_down):
    count, width = tokens.shape
    ff = w_gate.shape[2]
    half = count // HALVES
    wide = width + LANES
    cols = width // CHUNKS
    bf16 = jnp.bfloat16
    dma = pltpu.SemaphoreType.DMA
    each = (ROWS, HALVES, CHUNKS)
    return pl.pallas_call(
        fused_kernel,
        out_shape=jax.ShapeDtypeStruct((count, width), bf16),
        in_specs=[pl.BlockSpec(memory_space=pl.ANY)] * 6,
        out_specs=pl.BlockSpec(memory_space=pl.ANY),
        scratch_shapes=[
            pltpu.VMEM((ROWS, 2, 2, HALVES, half, wide), bf16),
            pltpu.VMEM(expert_ids.shape[::-1], jnp.int32),
            pltpu.VMEM(router_weights.shape[::-1], jnp.float32),
            pltpu.VMEM((HALVES, CHUNKS, half, cols), bf16),
            pltpu.VMEM((width, ff), bf16),
            pltpu.VMEM((width, ff), bf16),
            pltpu.VMEM((width, ff), bf16),
            pltpu.VMEM((4 * half, ff), bf16),
            pltpu.VMEM(each + (2, 2, half, cols), bf16),
            pltpu.VMEM(each + (2, half, cols), bf16),
            pltpu.VMEM(each + (half, cols), bf16),
            pltpu.VMEM(each + (half, cols), bf16),
            pltpu.VMEM(each + (half, cols), bf16),
            pltpu.VMEM((ROWS,) + each + (half, cols), bf16),
            dma((3,)), dma((3,)), dma((HALVES, CHUNKS)), dma((ROWS, 2, HALVES)), dma((ROWS, 2, HALVES)), dma(each), dma(each),
            dma((ROWS,) + each), dma((HALVES, 4)), dma((HALVES, 4)), dma((HALVES,)), dma((4,)),
        ],
        compiler_params=pltpu.CompilerParams(
            collective_id=0, has_side_effects=True, vmem_limit_bytes=60 * 1024 * 1024
        ),
        name="moe",
    )(tokens.reshape(HALVES, half, width), expert_ids.T, router_weights.T, w_gate, w_up, w_down)


def body(tokens, expert_ids, router_weights, w_gate, w_up, w_down):
    tok_count, top = expert_ids.shape
    experts = lax.axis_size("expert")
    cap = max(2, min(tok_count, 2 * tok_count * top // experts))
    args = (tokens, expert_ids, router_weights, w_gate, w_up, w_down)
    grid = experts == 4 * ROWS and lax.axis_size("dp") == 1 and tok_count % (16 * HALVES) == 0
    if cap >= tok_count and grid:
        return fused_body(*args)
    if cap >= tok_count:
        return dense_body(*args)
    return routed_body(cap, *args)


def solution(mesh):
    in_specs = (
        P(("parts", "expert", "dp"), None),
        P(("parts", "expert", "dp"), None),
        P(("parts", "expert", "dp"), None),
        P("expert", None, "dp"),
        P("expert", None, "dp"),
        P("expert", None, "dp"),
    )
    out_specs = P(("parts", "expert", "dp"), None)
    return jax.shard_map(body, mesh=mesh, in_specs=in_specs, out_specs=out_specs, check_vma=False)
```

```python
import functools
import math

import jax
import jax.numpy as jnp
from jax import lax
from jax.experimental import pallas as pl
from jax.experimental.pallas import tpu as pltpu
from jax.sharding import PartitionSpec as P

LANES = 128
PARTS = 3


def expert_rows(rows, gate_w, up_w, down_w):
    total = rows.shape[0]
    block = math.gcd(total, 128)
    pieces = []
    for index in range(total // block):
        block_rows = rows[index * block : (index + 1) * block]
        gate_val = jnp.dot(block_rows, gate_w, preferred_element_type=jnp.float32)
        up_val = jnp.dot(block_rows, up_w, preferred_element_type=jnp.float32)
        hidden = (jax.nn.silu(gate_val) * up_val).astype(jnp.bfloat16)
        pieces.append(
            lax.dot_general(
                hidden, down_w, (((1,), (1,)), ((), ())), preferred_element_type=jnp.float32
            )
        )
    return jnp.concatenate(pieces, 0)


def routed_body(cap, tokens, expert_ids, router_weights, w_gate, w_up, w_down):
    tok_count, top = expert_ids.shape
    width = tokens.shape[1]
    experts = lax.axis_size("expert")
    slots_all = experts * cap
    flat_ids = expert_ids.reshape(-1)
    onehot = (flat_ids[:, None] == jnp.arange(experts, dtype=jnp.int32)[None, :]).astype(jnp.int32)
    order = jnp.arange(flat_ids.shape[0], dtype=jnp.int32)
    earlier = (order[None, :] < order[:, None]).astype(jnp.bfloat16)
    before = jnp.dot(earlier, onehot.astype(jnp.bfloat16), preferred_element_type=jnp.float32).astype(jnp.int32)
    position = jnp.sum(before * onehot, 1)
    slot = flat_ids * cap + position
    send = jnp.zeros((slots_all, width), jnp.bfloat16).at[slot].set(jnp.repeat(tokens, top, 0))
    send = send.reshape(experts, cap, width)
    arrived = lax.all_to_all(send, "expert", split_axis=0, concat_axis=0, tiled=True)
    packed = arrived.reshape(slots_all, width)
    result = expert_rows(
        packed,
        lax.all_gather(w_gate, "dp", axis=2, tiled=True)[0],
        lax.all_gather(w_up, "dp", axis=2, tiled=True)[0],
        lax.all_gather(w_down, "dp", axis=2, tiled=True)[0],
    )
    expert_out = result.astype(jnp.bfloat16)
    back = lax.all_to_all(
        expert_out.reshape(experts, cap, width), "expert", split_axis=0, concat_axis=0, tiled=True
    )
    picked = back.reshape(slots_all, width)[slot].reshape(tok_count, top, width)
    mixed = jnp.einsum("tk,tkd->td", router_weights, picked.astype(jnp.float32))
    return mixed.astype(jnp.bfloat16)


def dense_body(tokens, expert_ids, router_weights, w_gate, w_up, w_down):
    experts = lax.axis_size("expert")
    axes = ("expert", "dp") if lax.axis_size("dp") > 1 else "expert"
    chosen = expert_ids[:, :, None] == jnp.arange(experts, dtype=jnp.int32)[None, None, :]
    table = jnp.sum(jnp.where(chosen, router_weights[:, :, None], 0.0), 1)
    table = lax.all_gather(table, axes, axis=0, tiled=True)
    rows = lax.all_gather(tokens, axes, axis=0, tiled=True)
    mine = jnp.arange(experts, dtype=jnp.int32)[None, :] == lax.axis_index("expert")
    weight = jnp.sum(jnp.where(mine, table, 0.0), 1, keepdims=True)
    gate_val = jnp.dot(rows, w_gate[0], preferred_element_type=jnp.float32)
    up_val = jnp.dot(rows, w_up[0], preferred_element_type=jnp.float32)
    hidden = (jax.nn.silu(gate_val) * up_val).astype(jnp.bfloat16)
    out = lax.dot_general(
        hidden, w_down[0], (((1,), (1,)), ((), ())), preferred_element_type=jnp.float32
    )
    part = (out * weight).astype(jnp.bfloat16)
    return lax.psum_scatter(part, axes, scatter_dimension=0, tiled=True)


MESH = pl.DeviceIdType.MESH
ROWS = 4
HALVES = 2
CHUNKS = 2
PIECES = 3
BLOCK = 512

EDGE = (
    ("W", 0, 0, 0), ("X", 0, 0), ("W", 0, 0, 1), ("Z", 0, 0, 0, 1), ("Z", 0, 0, 1, 1), ("X", 0, 1), ("W", 0, 1, 0),
    ("Z", 0, 1, 0, 1), ("W", 1, 0, 0), ("X", 1, 0), ("GU", 0, 0), ("GV", 0, 0, 1), ("W", 0, 1, 1), ("GV", 0, 0, 2),
    ("DN", 0, 0, 0), ("DN", 0, 0, 1), ("W", 2, 0, 0), ("X", 2, 0), ("GU", 0, 1), ("GV", 0, 1, 1), ("GV", 0, 1, 2),
    ("W", 1, 1, 0), ("DN", 0, 1, 0), ("DN", 0, 1, 1), ("W", 1, 0, 1), ("X", 1, 1), ("GU", 1, 0), ("GV", 1, 0, 1),
    ("GV", 1, 0, 2), ("W", 2, 1, 0), ("DN", 1, 0, 0), ("RX", 1, 0, 0), ("DN", 1, 0, 1), ("W", 3, 0, 0), ("X", 3, 0),
    ("GU", 2, 0), ("GV", 2, 0, 1), ("GV", 2, 0, 2), ("W", 1, 1, 1), ("FS", 1, 0, 0), ("DN", 2, 0, 0),
    ("DN", 2, 0, 1), ("GU", 1, 1), ("W", 3, 0, 1), ("X", 3, 1), ("RX", 2, 0, 0), ("RX", 0, 0, 0), ("GV", 1, 1, 1),
    ("GV", 1, 1, 2), ("W", 3, 1, 0), ("DN", 1, 1, 0), ("DN", 1, 1, 1), ("RX", 1, 0, 1), ("FS", 2, 0, 0),
    ("GU", 3, 0), ("GV", 3, 0, 1), ("RX", 1, 1, 0), ("GV", 3, 0, 2), ("DN", 3, 0, 0), ("W", 3, 1, 1),
    ("FS", 1, 1, 0), ("DN", 3, 0, 1), ("W", 2, 0, 1), ("RX", 3, 0, 0), ("RX", 2, 0, 1), ("GU", 3, 1),
    ("GV", 3, 1, 1), ("GV", 3, 1, 2), ("W", 2, 1, 1), ("DN", 3, 1, 0), ("RX", 3, 0, 1), ("DN", 3, 1, 1),
    ("FS", 3, 0, 0), ("GU", 2, 1), ("GV", 2, 1, 1), ("RX", 3, 1, 1), ("FS", 2, 0, 1), ("GV", 2, 1, 2),
    ("DN", 2, 1, 0), ("RX", 3, 1, 0), ("FS", 3, 0, 1), ("DN", 2, 1, 1), ("RX", 2, 1, 0), ("FS", 3, 1, 1),
    ("RX", 2, 1, 1), ("RX", 1, 1, 1), ("RX", 0, 1, 0), ("FS", 3, 1, 0), ("FS", 2, 1, 0), ("RX", 0, 1, 1),
    ("RX", 0, 0, 1), ("FS", 2, 1, 1), ("FS", 1, 0, 1), ("FS", 0, 0, 0), ("FS", 1, 1, 1), ("FS", 0, 1, 1),
    ("FS", 0, 1, 0), ("FS", 0, 0, 1),
)
INNER = (
    ("W", 1, 0, 0), ("Z", 1, 0, 0, 2), ("X", 1, 0), ("W", 1, 0, 1), ("Z", 1, 0, 1, 2), ("X", 1, 1),
    ("Z", 1, 0, 0, 0), ("W", 2, 0, 0), ("Z", 2, 0, 0, 0), ("W", 0, 0, 0), ("W", 1, 1, 0), ("Z", 0, 0, 0, 2),
    ("X", 2, 0), ("Z", 1, 0, 1, 0), ("GU", 1, 0), ("GV", 1, 0, 1), ("GV", 1, 0, 2), ("W", 0, 0, 1),
    ("Z", 0, 0, 1, 2), ("X", 0, 1), ("W", 3, 0, 0), ("Z", 3, 0, 0, 0), ("W", 0, 1, 0), ("DN", 1, 0, 0),
    ("DN", 1, 0, 1), ("Z", 0, 1, 0, 2), ("W", 2, 1, 0), ("GU", 0, 0), ("GV", 0, 0, 1), ("GV", 0, 0, 2),
    ("W", 1, 1, 1), ("W", 3, 0, 1), ("Z", 3, 0, 1, 0), ("DN", 0, 0, 0), ("DN", 0, 0, 1), ("W", 0, 1, 1),
    ("GU", 2, 0), ("GV", 2, 0, 1), ("Z", 1, 1, 1, 2), ("W", 2, 0, 1), ("Z", 2, 0, 1, 0), ("W", 3, 1, 0),
    ("GV", 2, 0, 2), ("X", 3, 1), ("DN", 2, 0, 0), ("DN", 2, 0, 1), ("GU", 0, 1), ("GV", 0, 1, 1), ("RX", 2, 0, 0),
    ("GV", 0, 1, 2), ("DN", 0, 1, 0), ("FS", 2, 0, 0), ("W", 2, 1, 1), ("RX", 0, 0, 0), ("Z", 2, 1, 1, 0),
    ("RX", 2, 0, 1), ("DN", 0, 1, 1), ("RX", 0, 0, 1), ("GU", 3, 0), ("GV", 3, 0, 1), ("GV", 3, 0, 2),
    ("W", 3, 1, 1), ("DN", 3, 0, 0), ("DN", 3, 0, 1), ("RX", 0, 1, 1), ("RX", 0, 1, 0), ("FS", 0, 1, 0),
    ("RX", 3, 0, 0), ("GU", 3, 1), ("RX", 1, 0, 1), ("RX", 3, 0, 1), ("GV", 3, 1, 1), ("GV", 3, 1, 2),
    ("DN", 3, 1, 0), ("FS", 3, 0, 1), ("DN", 3, 1, 1), ("GU", 2, 1), ("GV", 2, 1, 1), ("GV", 2, 1, 2),
    ("FS", 0, 0, 0), ("DN", 2, 1, 0), ("RX", 3, 1, 0), ("RX", 3, 1, 1), ("FS", 3, 0, 0), ("RX", 1, 0, 0),
    ("DN", 2, 1, 1), ("GU", 1, 1), ("GV", 1, 1, 1), ("FS", 2, 0, 1), ("GV", 1, 1, 2), ("DN", 1, 1, 0),
    ("RX", 2, 1, 0), ("FS", 0, 1, 1), ("DN", 1, 1, 1), ("FS", 3, 1, 1), ("RX", 2, 1, 1), ("RX", 1, 1, 0),
    ("RX", 1, 1, 1), ("FS", 3, 1, 0), ("FS", 1, 0, 0), ("FS", 2, 1, 0), ("FS", 0, 0, 1), ("FS", 2, 1, 1),
    ("FS", 1, 1, 0), ("FS", 1, 0, 1), ("FS", 1, 1, 1),
)
HOW = (
    (0, 1, 0, 0, 2),
    (0, 1, 1, 0, 2),
    (0, 2, 0, 0, 2),
    (0, 3, 0, 1, 1),
    (1, 0, 1, 0, 2),
    (1, 2, 0, 0, 2),
    (1, 3, 0, 0, 1),
    (1, 3, 0, 1, 2),
    (1, 3, 1, 0, 1),
    (1, 3, 1, 1, 1),
)


def way_of(n, s, h, q):
    key = (n, s, h, q) if n < ROWS // 2 else (ROWS - 1 - n, ROWS - 1 - s, h, q)
    return {item[:4]: item[4] for item in HOW}.get(key, 0)


def friendly(number):
    sizes = []
    while number:
        size = max(v for v in (16, 12, 8, 6, 4, 3, 2, 1) if v <= number)
        sizes.append(size)
        number -= size
    return sizes


def fused_kernel(
    token_ref, ids_hbm, scale_hbm, gate_hbm, up_hbm, down_hbm, out_hbm,
    tok, ids, scale, done, gate_w, up_w, down_w, hid, part, from_core, to_x, from_x, to_z, from_z, to_both, from_both,
    load_sem, own_sem, done_sem, ag_recv, agc_recv, rsc_recv, rsx_recv, rsz_recv, agz_send, agx_send, agc_send, other_send,
    rsx_send, rsz_send, rsb_send,
):
    me = lax.axis_index("expert")
    core = lax.rem(me, 2)
    col = lax.rem(me // 2, 2)
    row = me // 4
    width = token_ref.shape[2]
    half = tok.shape[4]
    cols = width // CHUNKS
    piece = gate_w.shape[1] // PIECES
    flip = row // 2
    edge = (row == 0) | (row == ROWS - 1)
    slab = [s + flip * (ROWS - 1 - 2 * s) for s in range(ROWS)]

    def device(r, x, c):
        return {"expert": (r * 2 + x) * 2 + c}

    partner = device(row, col, 1 - core)
    beside = device(row, 1 - col, core)

    loads = [
        pltpu.make_async_copy(gate_hbm.at[0], gate_w, load_sem.at[0]),
        pltpu.make_async_copy(up_hbm.at[0], up_w, load_sem.at[1]),
        pltpu.make_async_copy(down_hbm.at[0], down_w, load_sem.at[2]),
    ]
    owns = [
        pltpu.make_async_copy(ids_hbm, ids, own_sem.at[0]),
        pltpu.make_async_copy(scale_hbm, scale, own_sem.at[1]),
        pltpu.make_async_copy(token_ref, tok.at[row, core, col, :, :, pl.ds(0, width)], own_sem.at[2]),
    ]

    barrier = pltpu.get_barrier_semaphore()
    others = [partner, beside] + [device(lax.rem(row + n, ROWS), col, core) for n in range(1, ROWS)]
    for other in others:
        pl.semaphore_signal(barrier, inc=1, device_id=other, device_id_type=MESH)
    for own in owns:
        own.start()
    for load in loads:
        load.start()
    owns[0].wait()
    owns[1].wait()
    number = ROWS * 4
    kinds = lax.broadcasted_iota(jnp.int32, (number, 1), 0)
    left = jnp.zeros((number, HALVES * half), jnp.float32)
    for k in range(ids.shape[0]):
        left = left + jnp.where(ids[k : k + 1, :] == kinds, scale[k : k + 1, :], 0.0)
    terms = []
    for _ in range(PARTS):
        term = left.astype(jnp.bfloat16).astype(jnp.float32)
        left = left - term
        terms.append(term)
    terms = jnp.concatenate(terms, 0)
    span = LANES // HALVES
    line_at = lax.broadcasted_iota(jnp.int32, (PARTS * number, LANES), 0)
    lane_at = lax.broadcasted_iota(jnp.int32, (PARTS * number, LANES), 1)
    table = jnp.zeros((half, LANES), jnp.float32)
    for h in range(HALVES):
        move = jnp.where(lane_at == line_at + h * span, 1.0, 0.0)
        moved = lax.dot_general(terms, move, (((0,), (0,)), ((), ())), preferred_element_type=jnp.float32)
        table = table + moved[h * half : (h + 1) * half]
    tok[row, core, col, 0, :, width : width + LANES] = table.astype(jnp.bfloat16)
    pl.semaphore_wait(barrier, len(others))
    owns[2].wait()

    def remote(src, dst, send_sem, recv_sem, target):
        return pltpu.make_async_remote_copy(
            src_ref=src, dst_ref=dst, send_sem=send_sem, recv_sem=recv_sem,
            device_id=target, device_id_type=MESH,
        )

    def column(x):
        return 1 - col if x else col

    def chunk(s, c, x, h):
        return tok.at[s, c, x, h] if h == 0 else tok.at[s, c, x, h, :, pl.ds(0, width)]

    def token_copy(s, x, h, send_sem, target):
        block = chunk(slab[s], core, column(x), h)
        return remote(block, block, send_sem, ag_recv.at[slab[s], column(x), h], target)

    def token_core(s, x, h, mine):
        block = chunk(s, core if mine else 1 - core, x, h)
        return remote(block, block, agc_send.at[h], agc_recv.at[s, x, h], partner)

    def part_core(s, h, q):
        return remote(
            part.at[s, h, q, 1 - core], from_core.at[s, h, q], other_send, rsc_recv.at[s, h, q], partner
        )

    def sum_x(s, h, q, send_sem):
        return remote(to_x.at[s, h, q], from_x.at[s, h, q], send_sem, rsx_recv.at[s, h, q], beside)

    def sum_z(s, h, q, n, send_sem, target):
        return remote(to_z.at[s, h, q], from_z.at[n, s, h, q], send_sem, rsz_recv.at[n, s, h, q], target)

    def sum_both(s, h, q, n, send_sem, target):
        return remote(to_both.at[s, h, q], from_both.at[n, s, h, q], send_sem, rsz_recv.at[n, s, h, q], target)

    def core_sum(s, h, q, x):
        mine = part[s, h, q, core, x].astype(jnp.float32)
        return mine + from_core[s, h, q, x].astype(jnp.float32)

    def batch(size, h, sem):
        lead = size // 4 if size % 4 == 0 else size // 2 if size % 2 == 0 else size
        inner = size // lead
        block = tok.at[pl.ds(0, lead), pl.ds(0, max(1, inner // 2)), pl.ds(0, min(2, inner)), h]
        if h:
            block = block.at[:, :, :, :, pl.ds(0, width)]
        return pltpu.make_async_copy(block, block, sem)

    def batch_sums(ref, size, sem):
        lead = size // 4 if size % 4 == 0 else size // 2 if size % 2 == 0 else size
        inner = size // lead
        block = ref.at[pl.ds(0, lead), pl.ds(0, max(1, inner // 2)), pl.ds(0, min(2, inner))]
        return pltpu.make_async_copy(block, block, sem)

    class Line:
        def __init__(self, near, program):
            self.near = near
            self.program = program
            counts = {}
            for act in program:
                if act[0] in ("Z", "X"):
                    kind = (act[0], act[-1] if act[0] == "X" else act[3])
                    counts[kind] = counts.get(kind, 0) + 1
            self.sems = {}
            self.sizes = {}
            for kind, number in sorted(counts.items()):
                sem = agz_send if kind[0] == "Z" else agx_send
                self.sizes[kind] = friendly(number)
                self.sems[kind] = [
                    sem.at[kind[1], at] for at, size in enumerate(self.sizes[kind]) for _ in range(size)
                ]
            self.sums = {}
            for act in program:
                if act[0] in ("RX", "FS"):
                    kind = self.link(*act)
                    self.sums[kind] = self.sums.get(kind, 0) + 1
            self.sums.pop("")
            for kind, number in sorted(self.sums.items()):
                sem = {"x": rsx_send, "z": rsz_send, "b": rsb_send}[kind]
                self.sizes[kind] = friendly(number)
                self.sems[kind] = [sem.at[at] for at, size in enumerate(self.sizes[kind]) for _ in range(size)]
            self.slots = [[]]
            for act in program:
                if act[0] in ("GU", "GV", "DN"):
                    self.slots.append([])
                else:
                    self.slots[-1].append(act)
            self.order = [act[1:] for act in program if act[0] == "GU"]

        def toward(self, n):
            return device(slab[n], col, core)

        def run(self, at):
            for act in self.slots[at]:
                getattr(self, act[0])(*act[1:])

        def W(self, s, x, h):
            if not (s == self.near and x == 0):
                token_copy(s, x, h, agz_send.at[0, 0], beside).wait_recv()
            token_core(slab[s], column(x), h, True).start()

        def Z(self, s, x, h, n):
            token_copy(s, x, h, self.sems["Z", h].pop(), self.toward(n)).start()

        def X(self, s, h):
            token_copy(s, 0, h, self.sems["X", h].pop(), beside).start()

        def link(self, name, s, h, q):
            both = s != self.near and way_of(self.near, s, h, q) == 2
            if name == "RX":
                return "" if both else "x"
            return "" if s == self.near else "b" if both else "z"

        def RX(self, s, h, q):
            if not self.link("RX", s, h, q):
                return
            at = slab[s]
            part_core(at, h, q).wait_recv()
            total = core_sum(at, h, q, 1 - col)
            for n in range(ROWS):
                if s == self.near and n != s and way_of(n, s, h, q) == 2:
                    sum_both(at, h, q, slab[n], rsb_send.at[0], beside).wait_recv()
                    total = total + from_both[slab[n], at, h, q, 1 - col].astype(jnp.float32)
            to_x[at, h, q] = total.astype(jnp.bfloat16)
            sum_x(at, h, q, self.sems["x"].pop()).start()

        def FS(self, s, h, q):
            far = abs(self.near - s)
            at = slab[s]
            kind = self.link("FS", s, h, q)
            if kind == "b":
                part_core(at, h, q).wait_recv()
                total = core_sum(at, h, q, col)
                to_both[at, h, q, 1 - col] = core_sum(at, h, q, 1 - col).astype(jnp.bfloat16)
            else:
                sum_x(at, h, q, rsx_send.at[0]).wait_recv()
                total = core_sum(at, h, q, col) + from_x[at, h, q].astype(jnp.float32)
            for n in range(ROWS):
                how = way_of(n, s, h, q) if n != s else 0
                if far == 0 and how == 2:
                    total = total + from_both[slab[n], at, h, q, col].astype(jnp.float32)
                    continue
                beyond = abs(n - s) > far and (far == 0 or (n < self.near) == (self.near < s))
                if beyond and (how == 1 if far == 0 and abs(n - s) > 1 else how == 0 and abs(n - self.near) == 1):
                    sum_z(at, h, q, slab[n], rsz_send.at[0], beside).wait_recv()
                    total = total + from_z[slab[n], at, h, q].astype(jnp.float32)
            total = total.astype(jnp.bfloat16)
            if far == 0:
                done[h, q] = total
                self.store(h, q).start()
                return
            n = self.near - 1 if s < self.near else self.near + 1
            if way_of(self.near, s, h, q):
                n = s
            if kind == "b":
                to_both[at, h, q, col] = total
                sum_both(at, h, q, row, self.sems["b"].pop(), self.toward(n)).start()
            else:
                to_z[at, h, q] = total
                sum_z(at, h, q, row, self.sems["z"].pop(), self.toward(n)).start()

        def store(self, h, q):
            place = out_hbm.at[pl.ds(h * half, half), pl.ds(q * cols, cols)]
            return pltpu.make_async_copy(done.at[h, q], place, done_sem.at[h, q])

        def sent(self):
            for kind, sizes in self.sizes.items():
                if kind in self.sums:
                    ref, sem = {"x": (to_x, rsx_send), "z": (to_z, rsz_send), "b": (to_both, rsb_send)}[kind]
                    for at, size in enumerate(sizes):
                        batch_sums(ref, size, sem.at[at]).wait()
                    continue
                name, h = kind
                sem = agz_send if name == "Z" else agx_send
                for at, size in enumerate(sizes):
                    batch(size, h, sem.at[h, at]).wait()
            for h in range(HALVES):
                for q in range(CHUNKS):
                    self.store(h, q).wait()

    lines = [(edge, Line(0, EDGE)), (jnp.logical_not(edge), Line(1, INNER))]

    def hook(at):
        for here, line in lines:
            if line.slots[at]:
                pl.when(here)(functools.partial(line.run, at))

    lane = lax.broadcasted_iota(jnp.int32, (1, LANES), 1)

    def place(k):
        (s0, h0), (s1, h1) = lines[0][1].order[k], lines[1][1].order[k]
        s = slab[s0] if s0 == s1 else jnp.where(edge, slab[s0], slab[s1])
        return s, h0, h1

    at = 0
    for k in range(ROWS * HALVES):
        hook(at)
        s, h0, h1 = place(k)
        h = h0 if h0 == h1 else jnp.where(edge, h0, h1)
        if h0 == h1:
            for x in range(2):
                token_core(s, x, h0, False).wait_recv()
        else:
            for (here, _), mine in zip(lines, (h0, h1)):
                @pl.when(here)
                def _():
                    for x in range(2):
                        token_core(s, x, mine, False).wait_recv()
        pick = (lane // span == h) & (lane % span < PARTS * number) & (lane % number == me)
        tables = tok[s, :, :, 0, :, width : width + LANES].reshape(4 * half, LANES).astype(jnp.float32)
        weight = jnp.sum(jnp.where(pick, tables, 0.0), 1, keepdims=True)
        if k == 0:
            loads[0].wait()
            loads[1].wait()
        for j in range(PIECES):
            if j:
                hook(at)
            rows = tok[s, :, :, h, :, 0:width].reshape(4 * half, width)
            here = slice(j * piece, (j + 1) * piece)
            gate_val = jnp.dot(rows, gate_w[:, here], preferred_element_type=jnp.float32)
            up_val = jnp.dot(rows, up_w[:, here], preferred_element_type=jnp.float32)
            hid[:, here] = (gate_val / (1.0 + jnp.exp(-gate_val)) * up_val).astype(jnp.bfloat16)
            at += 1
        if k == 0:
            loads[2].wait()
        for q in range(CHUNKS):
            hook(at)
            for b in range(0, cols, BLOCK):
                value = lax.dot_general(
                    hid[...], down_w[q * cols + b : q * cols + b + BLOCK, :], (((1,), (1,)), ((), ())),
                    preferred_element_type=jnp.float32,
                )
                part[s, h, q, :, :, :, b : b + BLOCK] = (
                    (value * weight).astype(jnp.bfloat16).reshape(2, 2, half, BLOCK)
                )
            part_core(s, h, q).start()
            at += 1
    hook(at)

    for here, line in lines:
        pl.when(here)(line.sent)
    for h in range(HALVES):
        batch(2 * ROWS, h, agc_send.at[h]).wait()
    pltpu.make_async_copy(from_core, from_core, other_send).wait()


def fused_body(tokens, expert_ids, router_weights, w_gate, w_up, w_down):
    count, width = tokens.shape
    ff = w_gate.shape[2]
    half = count // HALVES
    wide = width + LANES
    cols = width // CHUNKS
    bf16 = jnp.bfloat16
    dma = pltpu.SemaphoreType.DMA
    each = (ROWS, HALVES, CHUNKS)
    return pl.pallas_call(
        fused_kernel,
        out_shape=pltpu.VMEM((count, width), bf16),
        in_specs=[pl.BlockSpec(memory_space=pl.ANY)] * 6,
        out_specs=pl.BlockSpec(memory_space=pl.ANY),
        scratch_shapes=[
            pltpu.VMEM((ROWS, 2, 2, HALVES, half, wide), bf16),
            pltpu.VMEM(expert_ids.shape[::-1], jnp.int32),
            pltpu.VMEM(router_weights.shape[::-1], jnp.float32),
            pltpu.VMEM((HALVES, CHUNKS, half, cols), bf16),
            pltpu.VMEM((width, ff), bf16),
            pltpu.VMEM((width, ff), bf16),
            pltpu.VMEM((width, ff), bf16),
            pltpu.VMEM((4 * half, ff), bf16),
            pltpu.VMEM(each + (2, 2, half, cols), bf16),
            pltpu.VMEM(each + (2, half, cols), bf16),
            pltpu.VMEM(each + (half, cols), bf16),
            pltpu.VMEM(each + (half, cols), bf16),
            pltpu.VMEM(each + (half, cols), bf16),
            pltpu.VMEM((ROWS,) + each + (half, cols), bf16),
            pltpu.VMEM(each + (2, half, cols), bf16),
            pltpu.VMEM((ROWS,) + each + (2, half, cols), bf16),
            dma((3,)), dma((3,)), dma((HALVES, CHUNKS)), dma((ROWS, 2, HALVES)), dma((ROWS, 2, HALVES)), dma(each), dma(each),
            dma((ROWS,) + each), dma((HALVES, 4)), dma((HALVES, 4)), dma((HALVES,)), dma,
            dma((4,)), dma((4,)), dma((4,)),
        ],
        compiler_params=pltpu.CompilerParams(
            collective_id=0, has_side_effects=True, vmem_limit_bytes=60 * 1024 * 1024
        ),
        name="moe",
    )(tokens.reshape(HALVES, half, width), expert_ids.T, router_weights.T, w_gate, w_up, w_down)


def body(tokens, expert_ids, router_weights, w_gate, w_up, w_down):
    tok_count, top = expert_ids.shape
    experts = lax.axis_size("expert")
    cap = max(2, min(tok_count, 2 * tok_count * top // experts))
    args = (tokens, expert_ids, router_weights, w_gate, w_up, w_down)
    grid = experts == 4 * ROWS and lax.axis_size("dp") == 1 and tok_count % (16 * HALVES) == 0
    grid = grid and w_gate.shape[2] % (PIECES * LANES) == 0 and tokens.shape[1] % (CHUNKS * BLOCK) == 0
    if cap >= tok_count and grid:
        return fused_body(*args)
    if cap >= tok_count:
        return dense_body(*args)
    return routed_body(cap, *args)


def solution(mesh):
    in_specs = (
        P(("parts", "expert", "dp"), None),
        P(("parts", "expert", "dp"), None),
        P(("parts", "expert", "dp"), None),
        P("expert", None, "dp"),
        P("expert", None, "dp"),
        P("expert", None, "dp"),
    )
    out_specs = P(("parts", "expert", "dp"), None)
    return jax.shard_map(body, mesh=mesh, in_specs=in_specs, out_specs=out_specs, check_vma=False)
```

```python
import functools
import math

import jax
import jax.numpy as jnp
from jax import lax
from jax.experimental import pallas as pl
from jax.experimental.pallas import tpu as pltpu
from jax.sharding import PartitionSpec as P

LANES = 128


def expert_rows(rows, gate_w, up_w, down_w):
    total = rows.shape[0]
    block = math.gcd(total, 128)
    pieces = []
    for index in range(total // block):
        block_rows = rows[index * block : (index + 1) * block]
        gate_val = jnp.dot(block_rows, gate_w, preferred_element_type=jnp.float32)
        up_val = jnp.dot(block_rows, up_w, preferred_element_type=jnp.float32)
        hidden = (jax.nn.silu(gate_val) * up_val).astype(jnp.bfloat16)
        pieces.append(
            lax.dot_general(
                hidden, down_w, (((1,), (1,)), ((), ())), preferred_element_type=jnp.float32
            )
        )
    return jnp.concatenate(pieces, 0)


def routed_body(cap, tokens, expert_ids, router_weights, w_gate, w_up, w_down):
    tok_count, top = expert_ids.shape
    width = tokens.shape[1]
    experts = lax.axis_size("expert")
    slots_all = experts * cap
    flat_ids = expert_ids.reshape(-1)
    onehot = (flat_ids[:, None] == jnp.arange(experts, dtype=jnp.int32)[None, :]).astype(jnp.int32)
    order = jnp.arange(flat_ids.shape[0], dtype=jnp.int32)
    earlier = (order[None, :] < order[:, None]).astype(jnp.bfloat16)
    before = jnp.dot(earlier, onehot.astype(jnp.bfloat16), preferred_element_type=jnp.float32).astype(jnp.int32)
    position = jnp.sum(before * onehot, 1)
    slot = flat_ids * cap + position
    send = jnp.zeros((slots_all, width), jnp.bfloat16).at[slot].set(jnp.repeat(tokens, top, 0))
    send = send.reshape(experts, cap, width)
    arrived = lax.all_to_all(send, "expert", split_axis=0, concat_axis=0, tiled=True)
    packed = arrived.reshape(slots_all, width)
    result = expert_rows(
        packed,
        lax.all_gather(w_gate, "dp", axis=2, tiled=True)[0],
        lax.all_gather(w_up, "dp", axis=2, tiled=True)[0],
        lax.all_gather(w_down, "dp", axis=2, tiled=True)[0],
    )
    expert_out = result.astype(jnp.bfloat16)
    back = lax.all_to_all(
        expert_out.reshape(experts, cap, width), "expert", split_axis=0, concat_axis=0, tiled=True
    )
    picked = back.reshape(slots_all, width)[slot].reshape(tok_count, top, width)
    mixed = jnp.einsum("tk,tkd->td", router_weights, picked.astype(jnp.float32))
    return mixed.astype(jnp.bfloat16)


def dense_body(tokens, expert_ids, router_weights, w_gate, w_up, w_down):
    experts = lax.axis_size("expert")
    axes = ("expert", "dp") if lax.axis_size("dp") > 1 else "expert"
    chosen = expert_ids[:, :, None] == jnp.arange(experts, dtype=jnp.int32)[None, None, :]
    table = jnp.sum(jnp.where(chosen, router_weights[:, :, None], 0.0), 1)
    table = lax.all_gather(table, axes, axis=0, tiled=True)
    rows = lax.all_gather(tokens, axes, axis=0, tiled=True)
    mine = jnp.arange(experts, dtype=jnp.int32)[None, :] == lax.axis_index("expert")
    weight = jnp.sum(jnp.where(mine, table, 0.0), 1, keepdims=True)
    gate_val = jnp.dot(rows, w_gate[0], preferred_element_type=jnp.float32)
    up_val = jnp.dot(rows, w_up[0], preferred_element_type=jnp.float32)
    hidden = (jax.nn.silu(gate_val) * up_val).astype(jnp.bfloat16)
    out = lax.dot_general(
        hidden, w_down[0], (((1,), (1,)), ((), ())), preferred_element_type=jnp.float32
    )
    part = (out * weight).astype(jnp.bfloat16)
    return lax.psum_scatter(part, axes, scatter_dimension=0, tiled=True)


MESH = pl.DeviceIdType.MESH
ROWS = 4
HALVES = 2
GROUPS = 4
CHUNKS = 2
PIECES = 3
BLOCK = 512
TERMS = 2
SIZES = (64, 48, 32, 24, 16, 12, 8, 6, 4, 3, 2, 1)

EDGE = (
    ("W", 0, 0, 0), ("X", 0, 0), ("Z", 0, 0, 0, 1), ("W", 0, 0, 3), ("W", 0, 0, 1), ("X", 0, 1), ("W", 0, 0, 2),
    ("Z", 0, 0, 1, 1), ("X", 0, 2), ("Z", 0, 0, 2, 1), ("W", 0, 1, 0), ("Z", 0, 0, 3, 1), ("X", 0, 3),
    ("Z", 0, 1, 0, 1), ("W", 0, 1, 1), ("W", 1, 0, 0), ("X", 1, 0), ("Z", 0, 1, 1, 1), ("W", 1, 0, 1), ("X", 1, 1),
    ("GU", 0, 0), ("W", 0, 1, 2), ("GV", 0, 0, 1), ("GV", 0, 0, 2), ("W", 0, 1, 3), ("DN", 0, 0, 0), ("W", 2, 0, 1),
    ("Z", 0, 1, 2, 1), ("X", 2, 1), ("DN", 0, 0, 1), ("W", 2, 0, 0), ("W", 1, 1, 0), ("GU", 0, 1), ("X", 2, 0),
    ("GV", 0, 1, 1), ("GV", 0, 1, 2), ("W", 1, 1, 1), ("DN", 0, 1, 0), ("DN", 0, 1, 1), ("W", 1, 1, 2),
    ("W", 3, 0, 0), ("X", 3, 0), ("GU", 1, 0), ("GV", 1, 0, 1), ("W", 2, 1, 1), ("W", 3, 0, 1), ("X", 3, 1),
    ("W", 2, 1, 0), ("GV", 1, 0, 2), ("DN", 1, 0, 0), ("W", 3, 0, 2), ("DN", 1, 0, 1), ("X", 3, 2), ("GU", 2, 0),
    ("W", 3, 1, 0), ("W", 3, 0, 3), ("RX", 1, 0, 0), ("RX", 1, 0, 1), ("GV", 2, 0, 1), ("X", 3, 3), ("GV", 2, 0, 2),
    ("RX", 0, 0, 1), ("W", 3, 1, 1), ("FS", 1, 0, 0), ("DN", 2, 0, 0), ("DN", 2, 0, 1), ("W", 1, 0, 2), ("GU", 3, 0),
    ("RX", 2, 0, 1), ("GV", 3, 0, 1), ("W", 3, 1, 2), ("RX", 2, 0, 0), ("GV", 3, 0, 2), ("W", 3, 1, 3),
    ("FS", 2, 0, 1), ("DN", 3, 0, 0), ("W", 1, 0, 3), ("DN", 3, 0, 1), ("GU", 3, 1), ("GV", 3, 1, 1),
    ("RX", 3, 0, 0), ("GV", 3, 1, 2), ("RX", 3, 0, 1), ("W", 1, 1, 3), ("FS", 2, 0, 0), ("W", 2, 1, 3),
    ("DN", 3, 1, 0), ("FS", 1, 0, 1), ("W", 2, 0, 2), ("DN", 3, 1, 1), ("GU", 1, 1), ("W", 2, 1, 2), ("RX", 3, 1, 0),
    ("GV", 1, 1, 1), ("FS", 3, 0, 0), ("RX", 3, 1, 1), ("W", 2, 0, 3), ("GV", 1, 1, 2), ("DN", 1, 1, 0),
    ("DN", 1, 1, 1), ("GU", 2, 1), ("GV", 2, 1, 1), ("RX", 1, 1, 0), ("FS", 3, 0, 1), ("GV", 2, 1, 2),
    ("RX", 1, 1, 1), ("DN", 2, 1, 0), ("DN", 2, 1, 1), ("FS", 3, 1, 0), ("RX", 2, 1, 1), ("FS", 3, 1, 1),
    ("RX", 2, 1, 0), ("FS", 1, 1, 0), ("RX", 0, 0, 0), ("RX", 0, 1, 1), ("FS", 2, 1, 1), ("RX", 0, 1, 0),
    ("FS", 2, 1, 0), ("FS", 1, 1, 1), ("FS", 0, 0, 0), ("FS", 0, 0, 1), ("FS", 0, 1, 1), ("FS", 0, 1, 0),
)
INNER = (
    ("W", 1, 0, 1), ("W", 1, 0, 2), ("Z", 1, 0, 1, 2), ("X", 1, 1), ("W", 1, 0, 0), ("X", 1, 0), ("Z", 1, 0, 0, 2),
    ("Z", 1, 0, 0, 0), ("X", 1, 2), ("W", 1, 0, 3), ("Z", 1, 0, 1, 0), ("X", 1, 3), ("W", 2, 0, 1), ("W", 0, 0, 0),
    ("Z", 2, 0, 1, 0), ("Z", 0, 0, 0, 2), ("W", 2, 0, 0), ("Z", 2, 0, 0, 0), ("W", 1, 1, 1), ("W", 0, 0, 1),
    ("Z", 0, 0, 1, 2), ("W", 1, 1, 0), ("X", 2, 1), ("W", 0, 0, 2), ("Z", 0, 0, 2, 2), ("W", 1, 1, 2),
    ("Z", 1, 1, 2, 0), ("GU", 1, 0), ("W", 3, 0, 0), ("X", 2, 0), ("Z", 3, 0, 0, 0), ("W", 0, 0, 3), ("X", 3, 0),
    ("W", 1, 1, 3), ("GV", 1, 0, 1), ("Z", 0, 0, 3, 2), ("X", 0, 3), ("GV", 1, 0, 2), ("Z", 1, 1, 3, 2),
    ("W", 3, 0, 1), ("Z", 3, 0, 1, 0), ("Z", 1, 0, 2, 2), ("W", 0, 1, 0), ("DN", 1, 0, 0), ("W", 3, 0, 2),
    ("Z", 3, 0, 2, 0), ("X", 3, 1), ("W", 0, 1, 1), ("W", 2, 1, 1), ("Z", 1, 1, 2, 2), ("X", 3, 2), ("DN", 1, 0, 1),
    ("W", 2, 1, 0), ("W", 3, 0, 3), ("Z", 3, 0, 3, 0), ("X", 3, 3), ("GU", 0, 0), ("W", 3, 1, 0), ("Z", 1, 0, 2, 0),
    ("GV", 0, 0, 1), ("GV", 0, 0, 2), ("W", 2, 1, 3), ("Z", 1, 0, 3, 0), ("W", 0, 1, 2), ("DN", 0, 0, 0),
    ("Z", 1, 1, 3, 0), ("RX", 0, 0, 0), ("W", 0, 1, 3), ("Z", 2, 1, 3, 0), ("DN", 0, 0, 1), ("W", 2, 0, 2),
    ("GU", 2, 0), ("GV", 2, 0, 1), ("GV", 2, 0, 2), ("RX", 0, 0, 1), ("Z", 1, 0, 3, 2), ("DN", 2, 0, 0),
    ("Z", 2, 0, 2, 0), ("DN", 2, 0, 1), ("GU", 0, 1), ("GV", 0, 1, 1), ("W", 2, 1, 2), ("W", 3, 1, 1),
    ("RX", 2, 0, 1), ("GV", 0, 1, 2), ("DN", 0, 1, 0), ("W", 2, 0, 3), ("Z", 2, 1, 2, 0), ("Z", 2, 0, 3, 0),
    ("RX", 2, 0, 0), ("DN", 0, 1, 1), ("GU", 3, 0), ("RX", 0, 1, 0), ("GV", 3, 0, 1), ("W", 3, 1, 3),
    ("GV", 3, 0, 2), ("FS", 2, 0, 1), ("FS", 0, 0, 1), ("DN", 3, 0, 0), ("RX", 1, 0, 0), ("RX", 0, 1, 1),
    ("DN", 3, 0, 1), ("FS", 2, 0, 0), ("GU", 2, 1), ("FS", 0, 0, 0), ("W", 3, 1, 2), ("GV", 2, 1, 1),
    ("GV", 2, 1, 2), ("DN", 2, 1, 0), ("RX", 2, 1, 0), ("RX", 3, 0, 0), ("DN", 2, 1, 1), ("GU", 3, 1),
    ("GV", 3, 1, 1), ("FS", 2, 1, 0), ("RX", 3, 0, 1), ("GV", 3, 1, 2), ("DN", 3, 1, 0), ("DN", 3, 1, 1),
    ("FS", 0, 1, 1), ("GU", 1, 1), ("RX", 3, 1, 0), ("FS", 3, 0, 0), ("FS", 1, 0, 0), ("RX", 3, 1, 1),
    ("GV", 1, 1, 1), ("RX", 1, 0, 1), ("FS", 3, 0, 1), ("RX", 2, 1, 1), ("FS", 3, 1, 0), ("GV", 1, 1, 2),
    ("DN", 1, 1, 0), ("FS", 3, 1, 1), ("DN", 1, 1, 1), ("RX", 1, 1, 0), ("RX", 1, 1, 1), ("FS", 0, 1, 0),
    ("FS", 1, 0, 1), ("FS", 2, 1, 1), ("FS", 1, 1, 0), ("FS", 1, 1, 1),
)
HOW = (
    (0, 1, 0, 0, 2),
    (0, 1, 0, 1, 2),
    (0, 2, 0, 0, 1),
    (0, 2, 0, 1, 2),
    (0, 2, 1, 0, 1),
    (1, 0, 0, 0, 2),
    (1, 2, 1, 0, 2),
    (1, 3, 0, 0, 1),
    (1, 3, 0, 1, 1),
    (1, 3, 1, 0, 1),
    (1, 3, 1, 1, 1),
)


def way_of(n, s, h, q):
    key = (n, s, h, q) if n < ROWS // 2 else (ROWS - 1 - n, ROWS - 1 - s, h, q)
    return {item[:4]: item[4] for item in HOW}.get(key, 0)


def friendly(number, most):
    sizes = []
    while number:
        size = max(v for v in SIZES if v <= min(number, most))
        sizes.append(size)
        number -= size
    return sizes


def fused_kernel(
    token_ref, ids_hbm, scale_hbm, gate_hbm, up_hbm, down_hbm, out_hbm,
    tok, ids, scale, done, gate_w, up_w, down_w, hid, part, from_core, to_x, from_x, to_z, from_z, to_both, from_both,
    load_sem, own_sem, done_sem, ag_recv, agc_recv, rsc_recv, rsx_recv, rsz_recv, agz_send, agx_send, agc_send, other_send,
    rsx_send, rsz_send, rsb_send,
):
    me = lax.axis_index("expert")
    core = lax.rem(me, 2)
    col = lax.rem(me // 2, 2)
    row = me // 4
    width = token_ref.shape[2]
    quarter = tok.shape[4]
    half = quarter * (GROUPS // HALVES)
    cols = width // CHUNKS
    piece = gate_w.shape[1] // PIECES
    flip = row // 2
    edge = (row == 0) | (row == ROWS - 1)
    slab = [s + flip * (ROWS - 1 - 2 * s) for s in range(ROWS)]

    def device(r, x, c):
        return {"expert": (r * 2 + x) * 2 + c}

    partner = device(row, col, 1 - core)
    beside = device(row, 1 - col, core)

    loads = [
        pltpu.make_async_copy(gate_hbm.at[0], gate_w, load_sem.at[0]),
        pltpu.make_async_copy(up_hbm.at[0], up_w, load_sem.at[1]),
        pltpu.make_async_copy(down_hbm.at[0], down_w, load_sem.at[2]),
    ]
    owns = [
        pltpu.make_async_copy(ids_hbm, ids, own_sem.at[0]),
        pltpu.make_async_copy(scale_hbm, scale, own_sem.at[1]),
        pltpu.make_async_copy(token_ref, tok.at[row, core, col, :, :, pl.ds(0, width)], own_sem.at[2]),
    ]

    barrier = pltpu.get_barrier_semaphore()
    others = [partner, beside] + [device(lax.rem(row + n, ROWS), col, core) for n in range(1, ROWS)]
    for other in others:
        pl.semaphore_signal(barrier, inc=1, device_id=other, device_id_type=MESH)
    for own in owns:
        own.start()
    for load in loads:
        load.start()
    owns[0].wait()
    owns[1].wait()
    number = ROWS * 4
    kinds = lax.broadcasted_iota(jnp.int32, (number, 1), 0)
    left = jnp.zeros((number, GROUPS * quarter), jnp.float32)
    for k in range(ids.shape[0]):
        left = left + jnp.where(ids[k : k + 1, :] == kinds, scale[k : k + 1, :], 0.0)
    terms = []
    for _ in range(TERMS):
        term = left.astype(jnp.bfloat16).astype(jnp.float32)
        left = left - term
        terms.append(term)
    terms = jnp.concatenate(terms, 0)
    span = LANES // GROUPS
    line_at = lax.broadcasted_iota(jnp.int32, (TERMS * number, LANES), 0)
    lane_at = lax.broadcasted_iota(jnp.int32, (TERMS * number, LANES), 1)
    table = jnp.zeros((quarter, LANES), jnp.float32)
    for h in range(GROUPS):
        move = jnp.where(lane_at == line_at + h * span, 1.0, 0.0)
        moved = lax.dot_general(terms, move, (((0,), (0,)), ((), ())), preferred_element_type=jnp.float32)
        table = table + moved[h * quarter : (h + 1) * quarter]
    tok[row, core, col, 0, :, width : width + LANES] = table.astype(jnp.bfloat16)
    pl.semaphore_wait(barrier, len(others))
    owns[2].wait()

    def remote(src, dst, send_sem, recv_sem, target):
        return pltpu.make_async_remote_copy(
            src_ref=src, dst_ref=dst, send_sem=send_sem, recv_sem=recv_sem,
            device_id=target, device_id_type=MESH,
        )

    def column(x):
        return 1 - col if x else col

    def chunk(s, c, x, h):
        return tok.at[s, c, x, h] if h == 0 else tok.at[s, c, x, h, :, pl.ds(0, width)]

    def token_copy(s, x, h, send_sem, target):
        block = chunk(slab[s], core, column(x), h)
        return remote(block, block, send_sem, ag_recv.at[slab[s], column(x), h], target)

    def token_core(s, x, h, mine):
        block = chunk(s, core if mine else 1 - core, x, h)
        return remote(block, block, agc_send.at[1 if h == 0 else 0], agc_recv.at[s, x, h], partner)

    def part_core(s, h, q):
        return remote(
            part.at[s, h, q, 1 - core], from_core.at[s, h, q], other_send, rsc_recv.at[s, h, q], partner
        )

    def sum_x(s, h, q, send_sem):
        return remote(to_x.at[s, h, q], from_x.at[s, h, q], send_sem, rsx_recv.at[s, h, q], beside)

    def sum_z(s, h, q, n, send_sem, target):
        return remote(to_z.at[s, h, q], from_z.at[n, s, h, q], send_sem, rsz_recv.at[n, s, h, q], target)

    def sum_both(s, h, q, n, send_sem, target):
        return remote(to_both.at[s, h, q], from_both.at[n, s, h, q], send_sem, rsz_recv.at[n, s, h, q], target)

    def core_sum(s, h, q, x):
        mine = part[s, h, q, core, x].astype(jnp.float32)
        return mine + from_core[s, h, q, x].astype(jnp.float32)

    def batch(size, wide, sem):
        fits = [
            (size // (b * c * d), b, c, d)
            for d in ((1,) if wide else (4, 2, 1)) for b, c in ((2, 2), (1, 2), (1, 1))
            if size % (b * c * d) == 0 and size // (b * c * d) <= ROWS
        ]
        a, b, c, d = fits[0]
        block = tok.at[pl.ds(0, a), pl.ds(0, b), pl.ds(0, c)]
        if wide:
            block = block.at[:, :, :, 0]
        else:
            block = block.at[:, :, :, pl.ds(0, d), :, pl.ds(0, width)]
        return pltpu.make_async_copy(block, block, sem)

    def batch_sums(ref, size, sem):
        lead = size // 4 if size % 4 == 0 else size // 2 if size % 2 == 0 else size
        inner = size // lead
        block = ref.at[pl.ds(0, lead), pl.ds(0, max(1, inner // 2)), pl.ds(0, min(2, inner))]
        return pltpu.make_async_copy(block, block, sem)

    class Line:
        def __init__(self, near, program):
            self.near = near
            self.program = program
            counts = {}
            for act in program:
                if act[0] in ("Z", "X"):
                    kind = (act[0], int((act[2] if act[0] == "X" else act[3]) == 0))
                    counts[kind] = counts.get(kind, 0) + 1
            self.sems = {}
            self.sizes = {}
            for kind, number in sorted(counts.items()):
                sem = agz_send if kind[0] == "Z" else agx_send
                self.sizes[kind] = friendly(number, 16 if kind[1] else 64)
                self.sems[kind] = [
                    sem.at[kind[1], at] for at, size in enumerate(self.sizes[kind]) for _ in range(size)
                ]
            self.sums = {}
            for act in program:
                if act[0] in ("RX", "FS"):
                    kind = self.link(*act)
                    self.sums[kind] = self.sums.get(kind, 0) + 1
            self.sums.pop("")
            for kind, number in sorted(self.sums.items()):
                sem = {"x": rsx_send, "z": rsz_send, "b": rsb_send}[kind]
                self.sizes[kind] = friendly(number, 16)
                self.sems[kind] = [sem.at[at] for at, size in enumerate(self.sizes[kind]) for _ in range(size)]
            self.slots = [[]]
            for act in program:
                if act[0] in ("GU", "GV", "DN"):
                    self.slots.append([])
                else:
                    self.slots[-1].append(act)
            self.order = [act[1:] for act in program if act[0] == "GU"]

        def toward(self, n):
            return device(slab[n], col, core)

        def run(self, at):
            for act in self.slots[at]:
                getattr(self, act[0])(*act[1:])

        def W(self, s, x, h):
            if not (s == self.near and x == 0):
                token_copy(s, x, h, agz_send.at[0, 0], beside).wait_recv()
            token_core(slab[s], column(x), h, True).start()

        def Z(self, s, x, h, n):
            token_copy(s, x, h, self.sems["Z", int(h == 0)].pop(), self.toward(n)).start()

        def X(self, s, h):
            token_copy(s, 0, h, self.sems["X", int(h == 0)].pop(), beside).start()

        def link(self, name, s, h, q):
            both = s != self.near and way_of(self.near, s, h, q) == 2
            if name == "RX":
                return "" if both else "x"
            return "" if s == self.near else "b" if both else "z"

        def RX(self, s, h, q):
            if not self.link("RX", s, h, q):
                return
            at = slab[s]
            part_core(at, h, q).wait_recv()
            total = core_sum(at, h, q, 1 - col)
            for n in range(ROWS):
                if s == self.near and n != s and way_of(n, s, h, q) == 2:
                    sum_both(at, h, q, slab[n], rsb_send.at[0], beside).wait_recv()
                    total = total + from_both[slab[n], at, h, q, 1 - col].astype(jnp.float32)
            to_x[at, h, q] = total.astype(jnp.bfloat16)
            sum_x(at, h, q, self.sems["x"].pop()).start()

        def FS(self, s, h, q):
            far = abs(self.near - s)
            at = slab[s]
            kind = self.link("FS", s, h, q)
            if kind == "b":
                part_core(at, h, q).wait_recv()
                total = core_sum(at, h, q, col)
                to_both[at, h, q, 1 - col] = core_sum(at, h, q, 1 - col).astype(jnp.bfloat16)
            else:
                sum_x(at, h, q, rsx_send.at[0]).wait_recv()
                total = core_sum(at, h, q, col) + from_x[at, h, q].astype(jnp.float32)
            for n in range(ROWS):
                how = way_of(n, s, h, q) if n != s else 0
                if far == 0 and how == 2:
                    total = total + from_both[slab[n], at, h, q, col].astype(jnp.float32)
                    continue
                beyond = abs(n - s) > far and (far == 0 or (n < self.near) == (self.near < s))
                if beyond and (how == 1 if far == 0 and abs(n - s) > 1 else how == 0 and abs(n - self.near) == 1):
                    sum_z(at, h, q, slab[n], rsz_send.at[0], beside).wait_recv()
                    total = total + from_z[slab[n], at, h, q].astype(jnp.float32)
            total = total.astype(jnp.bfloat16)
            if far == 0:
                done[h, q] = total
                self.store(h, q).start()
                return
            n = self.near - 1 if s < self.near else self.near + 1
            if way_of(self.near, s, h, q):
                n = s
            if kind == "b":
                to_both[at, h, q, col] = total
                sum_both(at, h, q, row, self.sems["b"].pop(), self.toward(n)).start()
            else:
                to_z[at, h, q] = total
                sum_z(at, h, q, row, self.sems["z"].pop(), self.toward(n)).start()

        def store(self, h, q):
            place = out_hbm.at[pl.ds(h * half, half), pl.ds(q * cols, cols)]
            return pltpu.make_async_copy(done.at[h, q], place, done_sem.at[h, q])

        def sent(self):
            for kind, sizes in self.sizes.items():
                if kind in self.sums:
                    ref, sem = {"x": (to_x, rsx_send), "z": (to_z, rsz_send), "b": (to_both, rsb_send)}[kind]
                    for at, size in enumerate(sizes):
                        batch_sums(ref, size, sem.at[at]).wait()
                    continue
                name, h = kind
                sem = agz_send if name == "Z" else agx_send
                for at, size in enumerate(sizes):
                    batch(size, h, sem.at[h, at]).wait()
            for h in range(HALVES):
                for q in range(CHUNKS):
                    self.store(h, q).wait()

    lines = [(edge, Line(0, EDGE)), (jnp.logical_not(edge), Line(1, INNER))]

    def hook(at):
        for here, line in lines:
            if line.slots[at]:
                pl.when(here)(functools.partial(line.run, at))

    lane = lax.broadcasted_iota(jnp.int32, (4, GROUPS // HALVES, quarter, LANES), 3)
    group = lax.broadcasted_iota(jnp.int32, (4, GROUPS // HALVES, quarter, LANES), 1)

    def place(k):
        (s0, h0), (s1, h1) = lines[0][1].order[k], lines[1][1].order[k]
        s = slab[s0] if s0 == s1 else jnp.where(edge, slab[s0], slab[s1])
        return s, h0, h1

    at = 0
    for k in range(ROWS * HALVES):
        hook(at)
        s, h0, h1 = place(k)
        h = h0 if h0 == h1 else jnp.where(edge, h0, h1)
        if h0 == h1:
            for x in range(2):
                for g in range(GROUPS // HALVES):
                    token_core(s, x, h0 * (GROUPS // HALVES) + g, False).wait_recv()
        else:
            for (here, _), mine in zip(lines, (h0, h1)):
                @pl.when(here)
                def _():
                    for x in range(2):
                        for g in range(GROUPS // HALVES):
                            token_core(s, x, mine * (GROUPS // HALVES) + g, False).wait_recv()
        tables = tok[s, :, :, 0, :, width : width + LANES].reshape(4, 1, quarter, LANES).astype(jnp.float32)
        tables = jnp.broadcast_to(tables, (4, GROUPS // HALVES, quarter, LANES))
        pick = (lane // span == group + h * (GROUPS // HALVES)) & (lane % number == me)
        weight = jnp.sum(jnp.where(pick, tables, 0.0).reshape(4 * half, LANES), 1, keepdims=True)
        if k == 0:
            loads[0].wait()
            loads[1].wait()
        for j in range(PIECES):
            if j:
                hook(at)
            rows = tok[s, :, :, pl.ds(h * (GROUPS // HALVES), GROUPS // HALVES), :, 0:width].reshape(4 * half, width)
            here = slice(j * piece, (j + 1) * piece)
            gate_val = jnp.dot(rows, gate_w[:, here], preferred_element_type=jnp.float32)
            up_val = jnp.dot(rows, up_w[:, here], preferred_element_type=jnp.float32)
            hid[:, here] = (gate_val / (1.0 + jnp.exp(-gate_val)) * up_val).astype(jnp.bfloat16)
            at += 1
        if k == 0:
            loads[2].wait()
        for q in range(CHUNKS):
            hook(at)
            for b in range(0, cols, BLOCK):
                value = lax.dot_general(
                    hid[...], down_w[q * cols + b : q * cols + b + BLOCK, :], (((1,), (1,)), ((), ())),
                    preferred_element_type=jnp.float32,
                )
                part[s, h, q, :, :, :, b : b + BLOCK] = (
                    (value * weight).astype(jnp.bfloat16).reshape(2, 2, half, BLOCK)
                )
            part_core(s, h, q).start()
            at += 1
    hook(at)

    for here, line in lines:
        pl.when(here)(line.sent)
    batch(2 * ROWS, 1, agc_send.at[1]).wait()
    batch(2 * ROWS * (GROUPS - 1), 0, agc_send.at[0]).wait()
    pltpu.make_async_copy(from_core, from_core, other_send).wait()


def fused_body(tokens, expert_ids, router_weights, w_gate, w_up, w_down):
    count, width = tokens.shape
    ff = w_gate.shape[2]
    half = count // HALVES
    wide = width + LANES
    cols = width // CHUNKS
    bf16 = jnp.bfloat16
    dma = pltpu.SemaphoreType.DMA
    each = (ROWS, HALVES, CHUNKS)
    return pl.pallas_call(
        fused_kernel,
        out_shape=pltpu.VMEM((count, width), bf16),
        in_specs=[pl.BlockSpec(memory_space=pl.ANY)] * 6,
        out_specs=pl.BlockSpec(memory_space=pl.ANY),
        scratch_shapes=[
            pltpu.VMEM((ROWS, 2, 2, GROUPS, count // GROUPS, wide), bf16),
            pltpu.VMEM(expert_ids.shape[::-1], jnp.int32),
            pltpu.VMEM(router_weights.shape[::-1], jnp.float32),
            pltpu.VMEM((HALVES, CHUNKS, half, cols), bf16),
            pltpu.VMEM((width, ff), bf16),
            pltpu.VMEM((width, ff), bf16),
            pltpu.VMEM((width, ff), bf16),
            pltpu.VMEM((4 * half, ff), bf16),
            pltpu.VMEM(each + (2, 2, half, cols), bf16),
            pltpu.VMEM(each + (2, half, cols), bf16),
            pltpu.VMEM(each + (half, cols), bf16),
            pltpu.VMEM(each + (half, cols), bf16),
            pltpu.VMEM(each + (half, cols), bf16),
            pltpu.VMEM((ROWS,) + each + (half, cols), bf16),
            pltpu.VMEM(each + (2, half, cols), bf16),
            pltpu.VMEM((ROWS,) + each + (2, half, cols), bf16),
            dma((3,)), dma((3,)), dma((HALVES, CHUNKS)), dma((ROWS, 2, GROUPS)), dma((ROWS, 2, GROUPS)), dma(each), dma(each),
            dma((ROWS,) + each), dma((HALVES, 4)), dma((HALVES, 4)), dma((HALVES,)), dma,
            dma((4,)), dma((4,)), dma((4,)),
        ],
        compiler_params=pltpu.CompilerParams(
            collective_id=0, has_side_effects=True, vmem_limit_bytes=60 * 1024 * 1024
        ),
        name="moe",
    )(tokens.reshape(GROUPS, count // GROUPS, width), expert_ids.T, router_weights.T, w_gate, w_up, w_down)


def body(tokens, expert_ids, router_weights, w_gate, w_up, w_down):
    tok_count, top = expert_ids.shape
    experts = lax.axis_size("expert")
    cap = max(2, min(tok_count, 2 * tok_count * top // experts))
    args = (tokens, expert_ids, router_weights, w_gate, w_up, w_down)
    grid = experts == 4 * ROWS and lax.axis_size("dp") == 1 and tok_count % (16 * GROUPS) == 0 and TERMS * experts * GROUPS <= LANES
    grid = grid and w_gate.shape[2] % (PIECES * LANES) == 0 and tokens.shape[1] % (CHUNKS * BLOCK) == 0
    if cap >= tok_count and grid:
        return fused_body(*args)
    if cap >= tok_count:
        return dense_body(*args)
    return routed_body(cap, *args)


def solution(mesh):
    in_specs = (
        P(("parts", "expert", "dp"), None),
        P(("parts", "expert", "dp"), None),
        P(("parts", "expert", "dp"), None),
        P("expert", None, "dp"),
        P("expert", None, "dp"),
        P("expert", None, "dp"),
    )
    out_specs = P(("parts", "expert", "dp"), None)
    return jax.shard_map(body, mesh=mesh, in_specs=in_specs, out_specs=out_specs, check_vma=False)
```

```python
import functools
import math

import jax
import jax.numpy as jnp
from jax import lax
from jax.experimental import pallas as pl
from jax.experimental.pallas import tpu as pltpu
from jax.sharding import PartitionSpec as P

LANES = 128


def expert_rows(rows, gate_w, up_w, down_w):
    total = rows.shape[0]
    block = math.gcd(total, 128)
    pieces = []
    for index in range(total // block):
        block_rows = rows[index * block : (index + 1) * block]
        gate_val = jnp.dot(block_rows, gate_w, preferred_element_type=jnp.float32)
        up_val = jnp.dot(block_rows, up_w, preferred_element_type=jnp.float32)
        hidden = (jax.nn.silu(gate_val) * up_val).astype(jnp.bfloat16)
        pieces.append(
            lax.dot_general(
                hidden, down_w, (((1,), (1,)), ((), ())), preferred_element_type=jnp.float32
            )
        )
    return jnp.concatenate(pieces, 0)


def routed_body(cap, tokens, expert_ids, router_weights, w_gate, w_up, w_down):
    tok_count, top = expert_ids.shape
    width = tokens.shape[1]
    experts = lax.axis_size("expert")
    slots_all = experts * cap
    flat_ids = expert_ids.reshape(-1)
    onehot = (flat_ids[:, None] == jnp.arange(experts, dtype=jnp.int32)[None, :]).astype(jnp.int32)
    order = jnp.arange(flat_ids.shape[0], dtype=jnp.int32)
    earlier = (order[None, :] < order[:, None]).astype(jnp.bfloat16)
    before = jnp.dot(earlier, onehot.astype(jnp.bfloat16), preferred_element_type=jnp.float32).astype(jnp.int32)
    position = jnp.sum(before * onehot, 1)
    slot = flat_ids * cap + position
    send = jnp.zeros((slots_all, width), jnp.bfloat16).at[slot].set(jnp.repeat(tokens, top, 0))
    send = send.reshape(experts, cap, width)
    arrived = lax.all_to_all(send, "expert", split_axis=0, concat_axis=0, tiled=True)
    packed = arrived.reshape(slots_all, width)
    result = expert_rows(
        packed,
        lax.all_gather(w_gate, "dp", axis=2, tiled=True)[0],
        lax.all_gather(w_up, "dp", axis=2, tiled=True)[0],
        lax.all_gather(w_down, "dp", axis=2, tiled=True)[0],
    )
    expert_out = result.astype(jnp.bfloat16)
    back = lax.all_to_all(
        expert_out.reshape(experts, cap, width), "expert", split_axis=0, concat_axis=0, tiled=True
    )
    picked = back.reshape(slots_all, width)[slot].reshape(tok_count, top, width)
    mixed = jnp.einsum("tk,tkd->td", router_weights, picked.astype(jnp.float32))
    return mixed.astype(jnp.bfloat16)


def dense_body(tokens, expert_ids, router_weights, w_gate, w_up, w_down):
    experts = lax.axis_size("expert")
    axes = ("expert", "dp") if lax.axis_size("dp") > 1 else "expert"
    chosen = expert_ids[:, :, None] == jnp.arange(experts, dtype=jnp.int32)[None, None, :]
    table = jnp.sum(jnp.where(chosen, router_weights[:, :, None], 0.0), 1)
    table = lax.all_gather(table, axes, axis=0, tiled=True)
    rows = lax.all_gather(tokens, axes, axis=0, tiled=True)
    mine = jnp.arange(experts, dtype=jnp.int32)[None, :] == lax.axis_index("expert")
    weight = jnp.sum(jnp.where(mine, table, 0.0), 1, keepdims=True)
    gate_val = jnp.dot(rows, w_gate[0], preferred_element_type=jnp.float32)
    up_val = jnp.dot(rows, w_up[0], preferred_element_type=jnp.float32)
    hidden = (jax.nn.silu(gate_val) * up_val).astype(jnp.bfloat16)
    out = lax.dot_general(
        hidden, w_down[0], (((1,), (1,)), ((), ())), preferred_element_type=jnp.float32
    )
    part = (out * weight).astype(jnp.bfloat16)
    return lax.psum_scatter(part, axes, scatter_dimension=0, tiled=True)


MESH = pl.DeviceIdType.MESH
ROWS = 4
HALVES = 2
GROUPS = 4
CHUNKS = 2
PIECES = 3
BLOCK = 512
TERMS = 2
SIZES = (64, 48, 32, 24, 16, 12, 8, 6, 4, 3, 2, 1)

EDGE = (
    ("W", 0, 0, 0), ("X", 0, 0), ("Z", 0, 0, 0, 1), ("W", 0, 0, 1), ("X", 0, 1), ("Z", 0, 0, 1, 1), ("W", 0, 0, 2),
    ("W", 0, 0, 3), ("Z", 0, 0, 2, 1), ("X", 0, 2), ("Z", 0, 0, 3, 1), ("W", 1, 0, 0), ("W", 0, 1, 0), ("X", 0, 3),
    ("W", 0, 1, 1), ("W", 1, 0, 1), ("Z", 0, 1, 1, 1), ("Z", 0, 1, 0, 1), ("X", 1, 0), ("GU", 0, 0), ("GV", 0, 0, 1),
    ("W", 0, 1, 2), ("GV", 0, 0, 2), ("W", 2, 0, 1), ("W", 0, 1, 3), ("DN", 0, 0, 0), ("X", 2, 1), ("DN", 0, 0, 1),
    ("W", 1, 1, 1), ("GU", 0, 1), ("GV", 0, 1, 1), ("W", 2, 0, 0), ("X", 2, 0), ("GV", 0, 1, 2), ("W", 1, 1, 0),
    ("DN", 0, 1, 0), ("DN", 0, 1, 1), ("W", 3, 0, 0), ("X", 3, 0), ("W", 2, 1, 1), ("GU", 1, 0), ("GV", 1, 0, 1),
    ("W", 3, 0, 1), ("X", 3, 1), ("GV", 1, 0, 2), ("W", 2, 1, 0), ("DN", 1, 0, 0), ("W", 3, 0, 2), ("X", 3, 2),
    ("DN", 1, 0, 1), ("GU", 2, 0), ("W", 3, 1, 0), ("RX", 1, 0, 0), ("GV", 2, 0, 1), ("FS", 1, 0, 0), ("W", 3, 0, 3),
    ("X", 3, 3), ("GV", 2, 0, 2), ("W", 3, 1, 1), ("DN", 2, 0, 0), ("DN", 2, 0, 1), ("W", 1, 0, 3), ("X", 1, 3),
    ("RX", 0, 0, 1), ("GU", 3, 0), ("GV", 3, 0, 1), ("W", 3, 1, 2), ("RX", 2, 0, 1), ("GV", 3, 0, 2),
    ("FS", 2, 0, 1), ("RX", 2, 0, 0), ("W", 3, 1, 3), ("RX", 1, 0, 1), ("DN", 3, 0, 0), ("FS", 1, 0, 1),
    ("W", 1, 0, 2), ("W", 1, 1, 2), ("DN", 3, 0, 1), ("GU", 3, 1), ("RX", 3, 0, 0), ("W", 1, 1, 3), ("GV", 3, 1, 1),
    ("GV", 3, 1, 2), ("W", 2, 0, 3), ("DN", 3, 1, 0), ("RX", 3, 0, 1), ("DN", 3, 1, 1), ("GU", 1, 1),
    ("GV", 1, 1, 1), ("FS", 2, 0, 0), ("RX", 3, 1, 0), ("GV", 1, 1, 2), ("W", 2, 1, 2), ("W", 2, 0, 2),
    ("W", 2, 1, 3), ("RX", 3, 1, 1), ("FS", 3, 0, 0), ("DN", 1, 1, 0), ("DN", 1, 1, 1), ("FS", 3, 0, 1),
    ("GU", 2, 1), ("GV", 2, 1, 1), ("RX", 1, 1, 0), ("GV", 2, 1, 2), ("DN", 2, 1, 0), ("DN", 2, 1, 1),
    ("RX", 1, 1, 1), ("FS", 3, 1, 0), ("FS", 3, 1, 1), ("RX", 2, 1, 1), ("RX", 2, 1, 0), ("RX", 0, 1, 0),
    ("FS", 1, 1, 0), ("FS", 2, 1, 1), ("RX", 0, 1, 1), ("FS", 2, 1, 0), ("RX", 0, 0, 0), ("FS", 1, 1, 1),
    ("FS", 0, 1, 1), ("FS", 0, 1, 0), ("FS", 0, 0, 1), ("FS", 0, 0, 0),
)
INNER = (
    ("W", 1, 0, 1), ("Z", 1, 0, 1, 2), ("W", 1, 0, 0), ("Z", 1, 0, 0, 0), ("X", 1, 1), ("X", 1, 0),
    ("Z", 1, 0, 0, 2), ("Z", 1, 0, 1, 0), ("W", 2, 0, 1), ("Z", 2, 0, 1, 0), ("X", 2, 1), ("W", 0, 0, 0),
    ("Z", 0, 0, 0, 2), ("W", 1, 1, 1), ("Z", 1, 1, 1, 0), ("W", 2, 0, 0), ("W", 1, 0, 3), ("X", 2, 0),
    ("W", 1, 1, 0), ("W", 0, 0, 1), ("Z", 0, 0, 1, 2), ("W", 1, 0, 2), ("X", 1, 3), ("Z", 2, 0, 0, 0),
    ("W", 0, 0, 2), ("Z", 0, 0, 2, 2), ("GU", 1, 0), ("GV", 1, 0, 1), ("X", 0, 2), ("W", 2, 1, 1), ("W", 3, 0, 0),
    ("Z", 3, 0, 0, 0), ("W", 0, 0, 3), ("X", 1, 2), ("Z", 0, 0, 3, 2), ("Z", 1, 0, 3, 2), ("X", 0, 3),
    ("GV", 1, 0, 2), ("W", 3, 0, 1), ("Z", 3, 0, 1, 0), ("W", 2, 1, 0), ("X", 3, 1), ("DN", 1, 0, 0),
    ("DN", 1, 0, 1), ("W", 3, 0, 2), ("Z", 3, 0, 2, 0), ("GU", 2, 0), ("GV", 2, 0, 1), ("Z", 1, 0, 2, 2),
    ("W", 3, 0, 3), ("W", 0, 1, 1), ("Z", 3, 0, 3, 0), ("X", 3, 3), ("W", 1, 1, 3), ("W", 0, 1, 0),
    ("Z", 1, 0, 3, 0), ("GV", 2, 0, 2), ("DN", 2, 0, 0), ("W", 1, 1, 2), ("Z", 1, 1, 2, 2), ("W", 0, 1, 2),
    ("X", 3, 0), ("DN", 2, 0, 1), ("GU", 0, 0), ("X", 3, 2), ("Z", 1, 1, 2, 0), ("Z", 1, 1, 3, 2), ("W", 0, 1, 3),
    ("Z", 1, 0, 2, 0), ("GV", 0, 0, 1), ("W", 2, 0, 2), ("Z", 2, 0, 2, 0), ("W", 2, 0, 3), ("W", 3, 1, 1),
    ("Z", 2, 0, 3, 0), ("RX", 2, 0, 1), ("GV", 0, 0, 2), ("DN", 0, 0, 0), ("W", 2, 1, 2), ("DN", 0, 0, 1),
    ("GU", 0, 1), ("W", 2, 1, 3), ("GV", 0, 1, 1), ("W", 3, 1, 3), ("GV", 0, 1, 2), ("RX", 0, 0, 1), ("DN", 0, 1, 0),
    ("DN", 0, 1, 1), ("RX", 0, 0, 0), ("W", 3, 1, 0), ("Z", 2, 1, 2, 0), ("GU", 2, 1), ("Z", 2, 1, 3, 0),
    ("GV", 2, 1, 1), ("RX", 0, 1, 1), ("FS", 2, 0, 1), ("RX", 2, 0, 0), ("RX", 1, 0, 0), ("GV", 2, 1, 2),
    ("DN", 2, 1, 0), ("DN", 2, 1, 1), ("RX", 2, 1, 0), ("GU", 3, 0), ("W", 3, 1, 2), ("FS", 0, 0, 0),
    ("RX", 0, 1, 0), ("GV", 3, 0, 1), ("GV", 3, 0, 2), ("DN", 3, 0, 0), ("FS", 2, 1, 0), ("FS", 0, 1, 1),
    ("DN", 3, 0, 1), ("GU", 3, 1), ("RX", 3, 0, 0), ("GV", 3, 1, 1), ("GV", 3, 1, 2), ("RX", 3, 0, 1),
    ("DN", 3, 1, 0), ("FS", 2, 0, 0), ("DN", 3, 1, 1), ("RX", 3, 1, 0), ("GU", 1, 1), ("FS", 3, 0, 0),
    ("RX", 3, 1, 1), ("GV", 1, 1, 1), ("RX", 1, 0, 1), ("GV", 1, 1, 2), ("FS", 3, 0, 1), ("FS", 0, 1, 0),
    ("DN", 1, 1, 0), ("RX", 2, 1, 1), ("DN", 1, 1, 1), ("FS", 3, 1, 0), ("FS", 1, 0, 0), ("FS", 3, 1, 1),
    ("FS", 0, 0, 1), ("RX", 1, 1, 0), ("RX", 1, 1, 1), ("FS", 1, 0, 1), ("FS", 2, 1, 1), ("FS", 1, 1, 0),
    ("FS", 1, 1, 1),
)
HOW = (
    (0, 1, 0, 0, 2),
    (0, 1, 0, 1, 2),
    (0, 2, 0, 1, 2),
    (0, 2, 1, 0, 1),
    (1, 0, 0, 0, 2),
    (1, 0, 1, 1, 2),
    (1, 2, 0, 1, 2),
    (1, 2, 1, 0, 2),
    (1, 3, 0, 0, 1),
    (1, 3, 1, 0, 1),
    (1, 3, 1, 1, 1),
)


def way_of(n, s, h, q):
    key = (n, s, h, q) if n < ROWS // 2 else (ROWS - 1 - n, ROWS - 1 - s, h, q)
    return {item[:4]: item[4] for item in HOW}.get(key, 0)


def friendly(number, most):
    sizes = []
    while number:
        size = max(v for v in SIZES if v <= min(number, most))
        sizes.append(size)
        number -= size
    return sizes


def fused_kernel(
    token_ref, ids_hbm, scale_hbm, gate_hbm, up_hbm, down_hbm, out_hbm,
    tok, ids, scale, done, gate_w, up_w, down_w, hid, part, from_core, to_x, from_x, to_z, from_z, to_both, from_both,
    load_sem, own_sem, done_sem, ag_recv, agc_recv, rsc_recv, rsx_recv, rsz_recv, agz_send, agx_send, agc_send, other_send,
    rsx_send, rsz_send, rsb_send,
):
    me = lax.axis_index("expert")
    core = lax.rem(me, 2)
    col = lax.rem(me // 2, 2)
    row = me // 4
    width = token_ref.shape[2]
    quarter = tok.shape[4]
    half = quarter * (GROUPS // HALVES)
    cols = width // CHUNKS
    piece = gate_w.shape[1] // PIECES
    flip = row // 2
    edge = (row == 0) | (row == ROWS - 1)
    slab = [s + flip * (ROWS - 1 - 2 * s) for s in range(ROWS)]

    def device(r, x, c):
        return {"expert": (r * 2 + x) * 2 + c}

    partner = device(row, col, 1 - core)
    beside = device(row, 1 - col, core)

    loads = [
        pltpu.make_async_copy(gate_hbm.at[0], gate_w, load_sem.at[0]),
        pltpu.make_async_copy(up_hbm.at[0], up_w, load_sem.at[1]),
        pltpu.make_async_copy(down_hbm.at[0], down_w, load_sem.at[2]),
    ]
    owns = [
        pltpu.make_async_copy(ids_hbm, ids, own_sem.at[0]),
        pltpu.make_async_copy(scale_hbm, scale, own_sem.at[1]),
        pltpu.make_async_copy(token_ref, tok.at[row, core, col, :, :, pl.ds(0, width)], own_sem.at[2]),
    ]

    barrier = pltpu.get_barrier_semaphore()
    others = [partner, beside] + [device(lax.rem(row + n, ROWS), col, core) for n in range(1, ROWS)]
    for other in others:
        pl.semaphore_signal(barrier, inc=1, device_id=other, device_id_type=MESH)
    for own in owns:
        own.start()
    for load in loads:
        load.start()
    owns[0].wait()
    owns[1].wait()
    number = ROWS * 4
    kinds = lax.broadcasted_iota(jnp.int32, (number, 1), 0)
    left = jnp.zeros((number, GROUPS * quarter), jnp.float32)
    for k in range(ids.shape[0]):
        left = left + jnp.where(ids[k : k + 1, :] == kinds, scale[k : k + 1, :], 0.0)
    terms = []
    for _ in range(TERMS):
        term = left.astype(jnp.bfloat16).astype(jnp.float32)
        left = left - term
        terms.append(term)
    terms = jnp.concatenate(terms, 0)
    span = LANES // GROUPS
    line_at = lax.broadcasted_iota(jnp.int32, (TERMS * number, LANES), 0)
    lane_at = lax.broadcasted_iota(jnp.int32, (TERMS * number, LANES), 1)
    table = jnp.zeros((quarter, LANES), jnp.float32)
    for h in range(GROUPS):
        move = jnp.where(lane_at == line_at + h * span, 1.0, 0.0)
        moved = lax.dot_general(terms, move, (((0,), (0,)), ((), ())), preferred_element_type=jnp.float32)
        table = table + moved[h * quarter : (h + 1) * quarter]
    tok[row, core, col, 0, :, width : width + LANES] = table.astype(jnp.bfloat16)
    pl.semaphore_wait(barrier, len(others))
    owns[2].wait()

    def remote(src, dst, send_sem, recv_sem, target):
        return pltpu.make_async_remote_copy(
            src_ref=src, dst_ref=dst, send_sem=send_sem, recv_sem=recv_sem,
            device_id=target, device_id_type=MESH,
        )

    def column(x):
        return 1 - col if x else col

    def chunk(s, c, x, h):
        return tok.at[s, c, x, h] if h == 0 else tok.at[s, c, x, h, :, pl.ds(0, width)]

    def token_copy(s, x, h, send_sem, target):
        block = chunk(slab[s], core, column(x), h)
        return remote(block, block, send_sem, ag_recv.at[slab[s], column(x), h], target)

    def token_core(s, x, h, mine):
        block = chunk(s, core if mine else 1 - core, x, h)
        return remote(block, block, agc_send.at[1 if h == 0 else 0], agc_recv.at[s, x, h], partner)

    def part_core(s, h, q):
        return remote(
            part.at[s, h, q, 1 - core], from_core.at[s, h, q], other_send, rsc_recv.at[s, h, q], partner
        )

    def sum_x(s, h, q, send_sem):
        return remote(to_x.at[s, h, q], from_x.at[s, h, q], send_sem, rsx_recv.at[s, h, q], beside)

    def sum_z(s, h, q, n, send_sem, target):
        return remote(to_z.at[s, h, q], from_z.at[n, s, h, q], send_sem, rsz_recv.at[n, s, h, q], target)

    def sum_both(s, h, q, n, send_sem, target):
        return remote(to_both.at[s, h, q], from_both.at[n, s, h, q], send_sem, rsz_recv.at[n, s, h, q], target)

    def core_sum(s, h, q, x):
        mine = part[s, h, q, core, x].astype(jnp.float32)
        return mine + from_core[s, h, q, x].astype(jnp.float32)

    def batch(size, wide, sem):
        fits = [
            (size // (b * c * d), b, c, d)
            for d in ((1,) if wide else (4, 2, 1)) for b, c in ((2, 2), (1, 2), (1, 1))
            if size % (b * c * d) == 0 and size // (b * c * d) <= ROWS
        ]
        a, b, c, d = fits[0]
        block = tok.at[pl.ds(0, a), pl.ds(0, b), pl.ds(0, c)]
        if wide:
            block = block.at[:, :, :, 0]
        else:
            block = block.at[:, :, :, pl.ds(0, d), :, pl.ds(0, width)]
        return pltpu.make_async_copy(block, block, sem)

    def batch_sums(ref, size, sem):
        lead = size // 4 if size % 4 == 0 else size // 2 if size % 2 == 0 else size
        inner = size // lead
        block = ref.at[pl.ds(0, lead), pl.ds(0, max(1, inner // 2)), pl.ds(0, min(2, inner))]
        return pltpu.make_async_copy(block, block, sem)

    class Line:
        def __init__(self, near, program):
            self.near = near
            self.program = program
            counts = {}
            for act in program:
                if act[0] in ("Z", "X"):
                    kind = (act[0], int((act[2] if act[0] == "X" else act[3]) == 0))
                    counts[kind] = counts.get(kind, 0) + 1
            self.sems = {}
            self.sizes = {}
            for kind, number in sorted(counts.items()):
                sem = agz_send if kind[0] == "Z" else agx_send
                self.sizes[kind] = friendly(number, 16 if kind[1] else 64)
                self.sems[kind] = [
                    sem.at[kind[1], at] for at, size in enumerate(self.sizes[kind]) for _ in range(size)
                ]
            self.sums = {}
            for act in program:
                if act[0] in ("RX", "FS"):
                    kind = self.link(*act)
                    self.sums[kind] = self.sums.get(kind, 0) + 1
            self.sums.pop("")
            for kind, number in sorted(self.sums.items()):
                sem = {"x": rsx_send, "z": rsz_send, "b": rsb_send}[kind]
                self.sizes[kind] = friendly(number, 16)
                self.sems[kind] = [sem.at[at] for at, size in enumerate(self.sizes[kind]) for _ in range(size)]
            self.slots = [[]]
            for act in program:
                if act[0] in ("GU", "GV", "DN"):
                    self.slots.append([])
                else:
                    self.slots[-1].append(act)
            self.order = [act[1:] for act in program if act[0] == "GU"]

        def toward(self, n):
            return device(slab[n], col, core)

        def run(self, at):
            for act in self.slots[at]:
                getattr(self, act[0])(*act[1:])

        def W(self, s, x, h):
            if not (s == self.near and x == 0):
                token_copy(s, x, h, agz_send.at[0, 0], beside).wait_recv()
            token_core(slab[s], column(x), h, True).start()

        def Z(self, s, x, h, n):
            token_copy(s, x, h, self.sems["Z", int(h == 0)].pop(), self.toward(n)).start()

        def X(self, s, h):
            token_copy(s, 0, h, self.sems["X", int(h == 0)].pop(), beside).start()

        def link(self, name, s, h, q):
            both = s != self.near and way_of(self.near, s, h, q) == 2
            if name == "RX":
                return "" if both else "x"
            return "" if s == self.near else "b" if both else "z"

        def RX(self, s, h, q):
            if not self.link("RX", s, h, q):
                return
            at = slab[s]
            part_core(at, h, q).wait_recv()
            total = core_sum(at, h, q, 1 - col)
            for n in range(ROWS):
                if s == self.near and n != s and way_of(n, s, h, q) == 2:
                    sum_both(at, h, q, slab[n], rsb_send.at[0], beside).wait_recv()
                    total = total + from_both[slab[n], at, h, q, 1 - col].astype(jnp.float32)
            to_x[at, h, q] = total.astype(jnp.bfloat16)
            sum_x(at, h, q, self.sems["x"].pop()).start()

        def FS(self, s, h, q):
            far = abs(self.near - s)
            at = slab[s]
            kind = self.link("FS", s, h, q)
            if kind == "b":
                part_core(at, h, q).wait_recv()
                total = core_sum(at, h, q, col)
                to_both[at, h, q, 1 - col] = core_sum(at, h, q, 1 - col).astype(jnp.bfloat16)
            else:
                sum_x(at, h, q, rsx_send.at[0]).wait_recv()
                total = core_sum(at, h, q, col) + from_x[at, h, q].astype(jnp.float32)
            for n in range(ROWS):
                how = way_of(n, s, h, q) if n != s else 0
                if far == 0 and how == 2:
                    total = total + from_both[slab[n], at, h, q, col].astype(jnp.float32)
                    continue
                beyond = abs(n - s) > far and (far == 0 or (n < self.near) == (self.near < s))
                if beyond and (how == 1 if far == 0 and abs(n - s) > 1 else how == 0 and abs(n - self.near) == 1):
                    sum_z(at, h, q, slab[n], rsz_send.at[0], beside).wait_recv()
                    total = total + from_z[slab[n], at, h, q].astype(jnp.float32)
            total = total.astype(jnp.bfloat16)
            if far == 0:
                done[h, q] = total
                self.store(h, q).start()
                return
            n = self.near - 1 if s < self.near else self.near + 1
            if way_of(self.near, s, h, q):
                n = s
            if kind == "b":
                to_both[at, h, q, col] = total
                sum_both(at, h, q, row, self.sems["b"].pop(), self.toward(n)).start()
            else:
                to_z[at, h, q] = total
                sum_z(at, h, q, row, self.sems["z"].pop(), self.toward(n)).start()

        def store(self, h, q):
            place = out_hbm.at[pl.ds(h * half, half), pl.ds(q * cols, cols)]
            return pltpu.make_async_copy(done.at[h, q], place, done_sem.at[h, q])

        def sent(self):
            for kind, sizes in self.sizes.items():
                if kind in self.sums:
                    ref, sem = {"x": (to_x, rsx_send), "z": (to_z, rsz_send), "b": (to_both, rsb_send)}[kind]
                    for at, size in enumerate(sizes):
                        batch_sums(ref, size, sem.at[at]).wait()
                    continue
                name, h = kind
                sem = agz_send if name == "Z" else agx_send
                for at, size in enumerate(sizes):
                    batch(size, h, sem.at[h, at]).wait()
            for h in range(HALVES):
                for q in range(CHUNKS):
                    self.store(h, q).wait()

    lines = [(edge, Line(0, EDGE)), (jnp.logical_not(edge), Line(1, INNER))]

    def hook(at):
        for here, line in lines:
            if line.slots[at]:
                pl.when(here)(functools.partial(line.run, at))

    lane = lax.broadcasted_iota(jnp.int32, (4, GROUPS // HALVES, quarter, LANES), 3)
    group = lax.broadcasted_iota(jnp.int32, (4, GROUPS // HALVES, quarter, LANES), 1)

    def place(k):
        (s0, h0), (s1, h1) = lines[0][1].order[k], lines[1][1].order[k]
        s = slab[s0] if s0 == s1 else jnp.where(edge, slab[s0], slab[s1])
        return s, h0, h1

    at = 0
    for k in range(ROWS * HALVES):
        hook(at)
        s, h0, h1 = place(k)
        h = h0 if h0 == h1 else jnp.where(edge, h0, h1)
        if h0 == h1:
            for x in range(2):
                for g in range(GROUPS // HALVES):
                    token_core(s, x, h0 * (GROUPS // HALVES) + g, False).wait_recv()
        else:
            for (here, _), mine in zip(lines, (h0, h1)):
                @pl.when(here)
                def _():
                    for x in range(2):
                        for g in range(GROUPS // HALVES):
                            token_core(s, x, mine * (GROUPS // HALVES) + g, False).wait_recv()
        tables = tok[s, :, :, 0, :, width : width + LANES].reshape(4, 1, quarter, LANES).astype(jnp.float32)
        tables = jnp.broadcast_to(tables, (4, GROUPS // HALVES, quarter, LANES))
        pick = (lane // span == group + h * (GROUPS // HALVES)) & (lane % number == me)
        weight = jnp.sum(jnp.where(pick, tables, 0.0).reshape(4 * half, LANES), 1, keepdims=True)
        if k == 0:
            loads[0].wait()
            loads[1].wait()
        for j in range(PIECES):
            if j:
                hook(at)
            rows = tok[s, :, :, pl.ds(h * (GROUPS // HALVES), GROUPS // HALVES), :, 0:width].reshape(4 * half, width)
            here = slice(j * piece, (j + 1) * piece)
            gate_val = jnp.dot(rows, gate_w[:, here], preferred_element_type=jnp.float32)
            up_val = jnp.dot(rows, up_w[:, here], preferred_element_type=jnp.float32)
            hid[:, here] = (gate_val / (1.0 + jnp.exp(-gate_val)) * up_val).astype(jnp.bfloat16)
            at += 1
        if k == 0:
            loads[2].wait()
        for q in range(CHUNKS):
            hook(at)
            for b in range(0, cols, BLOCK):
                value = lax.dot_general(
                    hid[...], down_w[q * cols + b : q * cols + b + BLOCK, :], (((1,), (1,)), ((), ())),
                    preferred_element_type=jnp.float32,
                )
                part[s, h, q, :, :, :, b : b + BLOCK] = (
                    (value * weight).astype(jnp.bfloat16).reshape(2, 2, half, BLOCK)
                )
            part_core(s, h, q).start()
            at += 1
    hook(at)

    for here, line in lines:
        pl.when(here)(line.sent)
    batch(2 * ROWS, 1, agc_send.at[1]).wait()
    batch(2 * ROWS * (GROUPS - 1), 0, agc_send.at[0]).wait()
    pltpu.make_async_copy(from_core, from_core, other_send).wait()


def fused_body(tokens, expert_ids, router_weights, w_gate, w_up, w_down):
    count, width = tokens.shape
    ff = w_gate.shape[2]
    half = count // HALVES
    wide = width + LANES
    cols = width // CHUNKS
    bf16 = jnp.bfloat16
    dma = pltpu.SemaphoreType.DMA
    each = (ROWS, HALVES, CHUNKS)
    return pl.pallas_call(
        fused_kernel,
        out_shape=pltpu.VMEM((count, width), bf16),
        in_specs=[pl.BlockSpec(memory_space=pl.ANY)] * 6,
        out_specs=pl.BlockSpec(memory_space=pl.ANY),
        scratch_shapes=[
            pltpu.VMEM((ROWS, 2, 2, GROUPS, count // GROUPS, wide), bf16),
            pltpu.VMEM(expert_ids.shape[::-1], jnp.int32),
            pltpu.VMEM(router_weights.shape[::-1], jnp.float32),
            pltpu.VMEM((HALVES, CHUNKS, half, cols), bf16),
            pltpu.VMEM((width, ff), bf16),
            pltpu.VMEM((width, ff), bf16),
            pltpu.VMEM((width, ff), bf16),
            pltpu.VMEM((4 * half, ff), bf16),
            pltpu.VMEM(each + (2, 2, half, cols), bf16),
            pltpu.VMEM(each + (2, half, cols), bf16),
            pltpu.VMEM(each + (half, cols), bf16),
            pltpu.VMEM(each + (half, cols), bf16),
            pltpu.VMEM(each + (half, cols), bf16),
            pltpu.VMEM((ROWS,) + each + (half, cols), bf16),
            pltpu.VMEM(each + (2, half, cols), bf16),
            pltpu.VMEM((ROWS,) + each + (2, half, cols), bf16),
            dma((3,)), dma((3,)), dma((HALVES, CHUNKS)), dma((ROWS, 2, GROUPS)), dma((ROWS, 2, GROUPS)), dma(each), dma(each),
            dma((ROWS,) + each), dma((HALVES, 4)), dma((HALVES, 4)), dma((HALVES,)), dma,
            dma((4,)), dma((4,)), dma((4,)),
        ],
        compiler_params=pltpu.CompilerParams(
            collective_id=0, has_side_effects=True, vmem_limit_bytes=60 * 1024 * 1024
        ),
        name="moe",
    )(tokens.reshape(GROUPS, count // GROUPS, width), expert_ids.T, router_weights.T, w_gate, w_up, w_down)


def body(tokens, expert_ids, router_weights, w_gate, w_up, w_down):
    tok_count, top = expert_ids.shape
    experts = lax.axis_size("expert")
    cap = max(2, min(tok_count, 2 * tok_count * top // experts))
    args = (tokens, expert_ids, router_weights, w_gate, w_up, w_down)
    grid = experts == 4 * ROWS and lax.axis_size("dp") == 1 and tok_count % (16 * GROUPS) == 0 and TERMS * experts * GROUPS <= LANES
    grid = grid and w_gate.shape[2] % (PIECES * LANES) == 0 and tokens.shape[1] % (CHUNKS * BLOCK) == 0
    if cap >= tok_count and grid:
        return fused_body(*args)
    if cap >= tok_count:
        return dense_body(*args)
    return routed_body(cap, *args)


def solution(mesh):
    in_specs = (
        P(("parts", "expert", "dp"), None),
        P(("parts", "expert", "dp"), None),
        P(("parts", "expert", "dp"), None),
        P("expert", None, "dp"),
        P("expert", None, "dp"),
        P("expert", None, "dp"),
    )
    out_specs = P(("parts", "expert", "dp"), None)
    return jax.shard_map(body, mesh=mesh, in_specs=in_specs, out_specs=out_specs, check_vma=False)
```

```python
import functools
import math

import jax
import jax.numpy as jnp
from jax import lax
from jax.experimental import pallas as pl
from jax.experimental.pallas import tpu as pltpu
from jax.sharding import PartitionSpec as P

LANES = 128


def expert_rows(rows, gate_w, up_w, down_w):
    total = rows.shape[0]
    block = math.gcd(total, 128)
    pieces = []
    for index in range(total // block):
        block_rows = rows[index * block : (index + 1) * block]
        gate_val = jnp.dot(block_rows, gate_w, preferred_element_type=jnp.float32)
        up_val = jnp.dot(block_rows, up_w, preferred_element_type=jnp.float32)
        hidden = (jax.nn.silu(gate_val) * up_val).astype(jnp.bfloat16)
        pieces.append(
            lax.dot_general(
                hidden, down_w, (((1,), (1,)), ((), ())), preferred_element_type=jnp.float32
            )
        )
    return jnp.concatenate(pieces, 0)


def routed_body(cap, tokens, expert_ids, router_weights, w_gate, w_up, w_down):
    tok_count, top = expert_ids.shape
    width = tokens.shape[1]
    experts = lax.axis_size("expert")
    slots_all = experts * cap
    flat_ids = expert_ids.reshape(-1)
    onehot = (flat_ids[:, None] == jnp.arange(experts, dtype=jnp.int32)[None, :]).astype(jnp.int32)
    order = jnp.arange(flat_ids.shape[0], dtype=jnp.int32)
    earlier = (order[None, :] < order[:, None]).astype(jnp.bfloat16)
    before = jnp.dot(earlier, onehot.astype(jnp.bfloat16), preferred_element_type=jnp.float32).astype(jnp.int32)
    position = jnp.sum(before * onehot, 1)
    slot = flat_ids * cap + position
    send = jnp.zeros((slots_all, width), jnp.bfloat16).at[slot].set(jnp.repeat(tokens, top, 0))
    send = send.reshape(experts, cap, width)
    arrived = lax.all_to_all(send, "expert", split_axis=0, concat_axis=0, tiled=True)
    packed = arrived.reshape(slots_all, width)
    result = expert_rows(
        packed,
        lax.all_gather(w_gate, "dp", axis=2, tiled=True)[0],
        lax.all_gather(w_up, "dp", axis=2, tiled=True)[0],
        lax.all_gather(w_down, "dp", axis=2, tiled=True)[0],
    )
    expert_out = result.astype(jnp.bfloat16)
    back = lax.all_to_all(
        expert_out.reshape(experts, cap, width), "expert", split_axis=0, concat_axis=0, tiled=True
    )
    picked = back.reshape(slots_all, width)[slot].reshape(tok_count, top, width)
    mixed = jnp.einsum("tk,tkd->td", router_weights, picked.astype(jnp.float32))
    return mixed.astype(jnp.bfloat16)


def dense_body(tokens, expert_ids, router_weights, w_gate, w_up, w_down):
    experts = lax.axis_size("expert")
    axes = ("expert", "dp") if lax.axis_size("dp") > 1 else "expert"
    chosen = expert_ids[:, :, None] == jnp.arange(experts, dtype=jnp.int32)[None, None, :]
    table = jnp.sum(jnp.where(chosen, router_weights[:, :, None], 0.0), 1)
    table = lax.all_gather(table, axes, axis=0, tiled=True)
    rows = lax.all_gather(tokens, axes, axis=0, tiled=True)
    mine = jnp.arange(experts, dtype=jnp.int32)[None, :] == lax.axis_index("expert")
    weight = jnp.sum(jnp.where(mine, table, 0.0), 1, keepdims=True)
    gate_val = jnp.dot(rows, w_gate[0], preferred_element_type=jnp.float32)
    up_val = jnp.dot(rows, w_up[0], preferred_element_type=jnp.float32)
    hidden = (jax.nn.silu(gate_val) * up_val).astype(jnp.bfloat16)
    out = lax.dot_general(
        hidden, w_down[0], (((1,), (1,)), ((), ())), preferred_element_type=jnp.float32
    )
    part = (out * weight).astype(jnp.bfloat16)
    return lax.psum_scatter(part, axes, scatter_dimension=0, tiled=True)


MESH = pl.DeviceIdType.MESH
ROWS = 4
HALVES = 2
GROUPS = 4
CHUNKS = 2
PIECES = 3
BLOCK = 512
TERMS = 2
SIZES = (64, 48, 32, 24, 16, 12, 8, 6, 4, 3, 2, 1)

EDGE = (
    ("W", 0, 0, 0), ("X", 0, 0), ("Z", 0, 0, 0, 1), ("W", 0, 0, 1), ("X", 0, 1), ("Z", 0, 0, 1, 1), ("W", 0, 0, 2),
    ("W", 0, 0, 3), ("Z", 0, 0, 2, 1), ("X", 0, 2), ("Z", 0, 0, 3, 1), ("W", 1, 0, 0), ("W", 0, 1, 0), ("X", 0, 3),
    ("W", 0, 1, 1), ("W", 1, 0, 1), ("Z", 0, 1, 1, 1), ("Z", 0, 1, 0, 1), ("X", 1, 0), ("GU", 0, 0), ("GV", 0, 0, 1),
    ("W", 0, 1, 2), ("GV", 0, 0, 2), ("W", 2, 0, 1), ("W", 0, 1, 3), ("DN", 0, 0, 0), ("X", 2, 1), ("DN", 0, 0, 1),
    ("W", 1, 1, 1), ("GU", 0, 1), ("GV", 0, 1, 1), ("W", 2, 0, 0), ("X", 2, 0), ("GV", 0, 1, 2), ("W", 1, 1, 0),
    ("DN", 0, 1, 0), ("DN", 0, 1, 1), ("W", 3, 0, 0), ("X", 3, 0), ("W", 2, 1, 1), ("GU", 1, 0), ("GV", 1, 0, 1),
    ("W", 3, 0, 1), ("X", 3, 1), ("GV", 1, 0, 2), ("W", 2, 1, 0), ("DN", 1, 0, 0), ("W", 3, 0, 2), ("X", 3, 2),
    ("DN", 1, 0, 1), ("GU", 2, 0), ("W", 3, 1, 0), ("RX", 1, 0, 0), ("GV", 2, 0, 1), ("FS", 1, 0, 0), ("W", 3, 0, 3),
    ("X", 3, 3), ("GV", 2, 0, 2), ("W", 3, 1, 1), ("DN", 2, 0, 0), ("DN", 2, 0, 1), ("W", 1, 0, 3), ("X", 1, 3),
    ("RX", 0, 0, 1), ("GU", 3, 0), ("GV", 3, 0, 1), ("W", 3, 1, 2), ("RX", 2, 0, 1), ("GV", 3, 0, 2),
    ("FS", 2, 0, 1), ("RX", 2, 0, 0), ("W", 3, 1, 3), ("RX", 1, 0, 1), ("DN", 3, 0, 0), ("FS", 1, 0, 1),
    ("W", 1, 0, 2), ("W", 1, 1, 2), ("DN", 3, 0, 1), ("GU", 3, 1), ("RX", 3, 0, 0), ("W", 1, 1, 3), ("GV", 3, 1, 1),
    ("GV", 3, 1, 2), ("W", 2, 0, 3), ("DN", 3, 1, 0), ("RX", 3, 0, 1), ("DN", 3, 1, 1), ("GU", 1, 1),
    ("GV", 1, 1, 1), ("FS", 2, 0, 0), ("RX", 3, 1, 0), ("GV", 1, 1, 2), ("W", 2, 1, 2), ("W", 2, 0, 2),
    ("W", 2, 1, 3), ("RX", 3, 1, 1), ("FS", 3, 0, 0), ("DN", 1, 1, 0), ("DN", 1, 1, 1), ("FS", 3, 0, 1),
    ("GU", 2, 1), ("GV", 2, 1, 1), ("RX", 1, 1, 0), ("GV", 2, 1, 2), ("DN", 2, 1, 0), ("DN", 2, 1, 1),
    ("RX", 1, 1, 1), ("FS", 3, 1, 0), ("FS", 3, 1, 1), ("RX", 2, 1, 1), ("RX", 2, 1, 0), ("RX", 0, 1, 0),
    ("FS", 1, 1, 0), ("FS", 2, 1, 1), ("RX", 0, 1, 1), ("FS", 2, 1, 0), ("RX", 0, 0, 0), ("FS", 1, 1, 1),
    ("FS", 0, 1, 1), ("FS", 0, 1, 0), ("FS", 0, 0, 1), ("FS", 0, 0, 0),
)
INNER = (
    ("W", 1, 0, 1), ("Z", 1, 0, 1, 2), ("W", 1, 0, 0), ("Z", 1, 0, 0, 0), ("X", 1, 1), ("X", 1, 0),
    ("Z", 1, 0, 0, 2), ("Z", 1, 0, 1, 0), ("W", 2, 0, 1), ("Z", 2, 0, 1, 0), ("X", 2, 1), ("W", 0, 0, 0),
    ("Z", 0, 0, 0, 2), ("W", 1, 1, 1), ("Z", 1, 1, 1, 0), ("W", 2, 0, 0), ("W", 1, 0, 3), ("X", 2, 0),
    ("W", 1, 1, 0), ("W", 0, 0, 1), ("Z", 0, 0, 1, 2), ("W", 1, 0, 2), ("X", 1, 3), ("Z", 2, 0, 0, 0),
    ("W", 0, 0, 2), ("Z", 0, 0, 2, 2), ("GU", 1, 0), ("GV", 1, 0, 1), ("X", 0, 2), ("W", 2, 1, 1), ("W", 3, 0, 0),
    ("Z", 3, 0, 0, 0), ("W", 0, 0, 3), ("X", 1, 2), ("Z", 0, 0, 3, 2), ("Z", 1, 0, 3, 2), ("X", 0, 3),
    ("GV", 1, 0, 2), ("W", 3, 0, 1), ("Z", 3, 0, 1, 0), ("W", 2, 1, 0), ("X", 3, 1), ("DN", 1, 0, 0),
    ("DN", 1, 0, 1), ("W", 3, 0, 2), ("Z", 3, 0, 2, 0), ("GU", 2, 0), ("GV", 2, 0, 1), ("Z", 1, 0, 2, 2),
    ("W", 3, 0, 3), ("W", 0, 1, 1), ("Z", 3, 0, 3, 0), ("X", 3, 3), ("W", 1, 1, 3), ("W", 0, 1, 0),
    ("Z", 1, 0, 3, 0), ("GV", 2, 0, 2), ("DN", 2, 0, 0), ("W", 1, 1, 2), ("Z", 1, 1, 2, 2), ("W", 0, 1, 2),
    ("X", 3, 0), ("DN", 2, 0, 1), ("GU", 0, 0), ("X", 3, 2), ("Z", 1, 1, 2, 0), ("Z", 1, 1, 3, 2), ("W", 0, 1, 3),
    ("Z", 1, 0, 2, 0), ("GV", 0, 0, 1), ("W", 2, 0, 2), ("Z", 2, 0, 2, 0), ("W", 2, 0, 3), ("W", 3, 1, 1),
    ("Z", 2, 0, 3, 0), ("RX", 2, 0, 1), ("GV", 0, 0, 2), ("DN", 0, 0, 0), ("W", 2, 1, 2), ("DN", 0, 0, 1),
    ("GU", 0, 1), ("W", 2, 1, 3), ("GV", 0, 1, 1), ("W", 3, 1, 3), ("GV", 0, 1, 2), ("RX", 0, 0, 1), ("DN", 0, 1, 0),
    ("DN", 0, 1, 1), ("RX", 0, 0, 0), ("W", 3, 1, 0), ("Z", 2, 1, 2, 0), ("GU", 2, 1), ("Z", 2, 1, 3, 0),
    ("GV", 2, 1, 1), ("RX", 0, 1, 1), ("FS", 2, 0, 1), ("RX", 2, 0, 0), ("RX", 1, 0, 0), ("GV", 2, 1, 2),
    ("DN", 2, 1, 0), ("DN", 2, 1, 1), ("RX", 2, 1, 0), ("GU", 3, 0), ("W", 3, 1, 2), ("FS", 0, 0, 0),
    ("RX", 0, 1, 0), ("GV", 3, 0, 1), ("GV", 3, 0, 2), ("DN", 3, 0, 0), ("FS", 2, 1, 0), ("FS", 0, 1, 1),
    ("DN", 3, 0, 1), ("GU", 3, 1), ("RX", 3, 0, 0), ("GV", 3, 1, 1), ("GV", 3, 1, 2), ("RX", 3, 0, 1),
    ("DN", 3, 1, 0), ("FS", 2, 0, 0), ("DN", 3, 1, 1), ("RX", 3, 1, 0), ("GU", 1, 1), ("FS", 3, 0, 0),
    ("RX", 3, 1, 1), ("GV", 1, 1, 1), ("RX", 1, 0, 1), ("GV", 1, 1, 2), ("FS", 3, 0, 1), ("FS", 0, 1, 0),
    ("DN", 1, 1, 0), ("RX", 2, 1, 1), ("DN", 1, 1, 1), ("FS", 3, 1, 0), ("FS", 1, 0, 0), ("FS", 3, 1, 1),
    ("FS", 0, 0, 1), ("RX", 1, 1, 0), ("RX", 1, 1, 1), ("FS", 1, 0, 1), ("FS", 2, 1, 1), ("FS", 1, 1, 0),
    ("FS", 1, 1, 1),
)
HOW = (
    (0, 1, 0, 0, 2),
    (0, 1, 0, 1, 2),
    (0, 2, 0, 1, 2),
    (0, 2, 1, 0, 1),
    (1, 0, 0, 0, 2),
    (1, 0, 1, 1, 2),
    (1, 2, 0, 1, 2),
    (1, 2, 1, 0, 2),
    (1, 3, 0, 0, 1),
    (1, 3, 1, 0, 1),
    (1, 3, 1, 1, 1),
)


def way_of(n, s, h, q):
    key = (n, s, h, q) if n < ROWS // 2 else (ROWS - 1 - n, ROWS - 1 - s, h, q)
    return {item[:4]: item[4] for item in HOW}.get(key, 0)


def friendly(number, most):
    sizes = []
    while number:
        size = max(v for v in SIZES if v <= min(number, most))
        sizes.append(size)
        number -= size
    return sizes


def fused_kernel(
    token_ref, ids_hbm, scale_hbm, gate_hbm, up_hbm, down_hbm, out_ref,
    tok, ids, scale, gate_w, up_w, down_w, hid, part, from_core, to_x, from_x, to_z, from_z, to_both, from_both,
    load_sem, own_sem, ag_recv, agc_recv, rsc_recv, rsx_recv, rsz_recv, agz_send, agx_send, agc_send, other_send,
    rsx_send, rsz_send, rsb_send,
):
    me = lax.axis_index("expert")
    core = lax.rem(me, 2)
    col = lax.rem(me // 2, 2)
    row = me // 4
    width = token_ref.shape[2]
    quarter = tok.shape[4]
    half = quarter * (GROUPS // HALVES)
    cols = width // CHUNKS
    piece = gate_w.shape[1] // PIECES
    flip = row // 2
    edge = (row == 0) | (row == ROWS - 1)
    slab = [s + flip * (ROWS - 1 - 2 * s) for s in range(ROWS)]

    def device(r, x, c):
        return {"expert": (r * 2 + x) * 2 + c}

    partner = device(row, col, 1 - core)
    beside = device(row, 1 - col, core)

    loads = [
        pltpu.make_async_copy(gate_hbm.at[0], gate_w, load_sem.at[0]),
        pltpu.make_async_copy(up_hbm.at[0], up_w, load_sem.at[1]),
        pltpu.make_async_copy(down_hbm.at[0], down_w, load_sem.at[2]),
    ]
    owns = [
        pltpu.make_async_copy(ids_hbm, ids, own_sem.at[0]),
        pltpu.make_async_copy(scale_hbm, scale, own_sem.at[1]),
        pltpu.make_async_copy(token_ref, tok.at[row, core, col, :, :, pl.ds(0, width)], own_sem.at[2]),
    ]

    for own in reversed(owns):
        own.start()
    barrier = pltpu.get_barrier_semaphore()
    others = [partner, beside] + [device(lax.rem(row + n, ROWS), col, core) for n in range(1, ROWS)]
    for other in others:
        pl.semaphore_signal(barrier, inc=1, device_id=other, device_id_type=MESH)
    for load in loads:
        load.start()
    owns[0].wait()
    owns[1].wait()
    number = ROWS * 4
    kinds = lax.broadcasted_iota(jnp.int32, (number, 1), 0)
    left = jnp.zeros((number, GROUPS * quarter), jnp.float32)
    for k in range(ids.shape[0]):
        left = left + jnp.where(ids[k : k + 1, :] == kinds, scale[k : k + 1, :], 0.0)
    terms = []
    for _ in range(TERMS):
        term = left.astype(jnp.bfloat16).astype(jnp.float32)
        left = left - term
        terms.append(term)
    terms = jnp.concatenate(terms, 0)
    span = LANES // GROUPS
    line_at = lax.broadcasted_iota(jnp.int32, (TERMS * number, LANES), 0)
    lane_at = lax.broadcasted_iota(jnp.int32, (TERMS * number, LANES), 1)
    table = jnp.zeros((quarter, LANES), jnp.float32)
    for h in range(GROUPS):
        move = jnp.where(lane_at == line_at + h * span, 1.0, 0.0)
        moved = lax.dot_general(terms, move, (((0,), (0,)), ((), ())), preferred_element_type=jnp.float32)
        table = table + moved[h * quarter : (h + 1) * quarter]
    tok[row, core, col, 0, :, width : width + LANES] = table.astype(jnp.bfloat16)
    pl.semaphore_wait(barrier, len(others))
    owns[2].wait()

    def remote(src, dst, send_sem, recv_sem, target):
        return pltpu.make_async_remote_copy(
            src_ref=src, dst_ref=dst, send_sem=send_sem, recv_sem=recv_sem,
            device_id=target, device_id_type=MESH,
        )

    def column(x):
        return 1 - col if x else col

    def chunk(s, c, x, h):
        return tok.at[s, c, x, h] if h == 0 else tok.at[s, c, x, h, :, pl.ds(0, width)]

    def token_copy(s, x, h, send_sem, target):
        block = chunk(slab[s], core, column(x), h)
        return remote(block, block, send_sem, ag_recv.at[slab[s], column(x), h], target)

    def token_core(s, x, h, mine):
        block = chunk(s, core if mine else 1 - core, x, h)
        return remote(block, block, agc_send.at[1 if h == 0 else 0], agc_recv.at[s, x, h], partner)

    def part_core(s, h, q):
        return remote(
            part.at[s, h, q, 1 - core], from_core.at[s, h, q], other_send, rsc_recv.at[s, h, q], partner
        )

    def sum_x(s, h, q, send_sem):
        return remote(to_x.at[s, h, q], from_x.at[s, h, q], send_sem, rsx_recv.at[s, h, q], beside)

    def sum_z(s, h, q, n, send_sem, target):
        return remote(to_z.at[s, h, q], from_z.at[n, s, h, q], send_sem, rsz_recv.at[n, s, h, q], target)

    def sum_both(s, h, q, n, send_sem, target):
        return remote(to_both.at[s, h, q], from_both.at[n, s, h, q], send_sem, rsz_recv.at[n, s, h, q], target)

    def core_sum(s, h, q, x):
        mine = part[s, h, q, core, x].astype(jnp.float32)
        return mine + from_core[s, h, q, x].astype(jnp.float32)

    def batch(size, wide, sem):
        fits = [
            (size // (b * c * d), b, c, d)
            for d in ((1,) if wide else (4, 2, 1)) for b, c in ((2, 2), (1, 2), (1, 1))
            if size % (b * c * d) == 0 and size // (b * c * d) <= ROWS
        ]
        a, b, c, d = fits[0]
        block = tok.at[pl.ds(0, a), pl.ds(0, b), pl.ds(0, c)]
        if wide:
            block = block.at[:, :, :, 0]
        else:
            block = block.at[:, :, :, pl.ds(0, d), :, pl.ds(0, width)]
        return pltpu.make_async_copy(block, block, sem)

    def batch_sums(ref, size, sem):
        lead = size // 4 if size % 4 == 0 else size // 2 if size % 2 == 0 else size
        inner = size // lead
        block = ref.at[pl.ds(0, lead), pl.ds(0, max(1, inner // 2)), pl.ds(0, min(2, inner))]
        return pltpu.make_async_copy(block, block, sem)

    class Line:
        def __init__(self, near, program):
            self.near = near
            self.program = program
            counts = {}
            for act in program:
                if act[0] in ("Z", "X"):
                    kind = (act[0], int((act[2] if act[0] == "X" else act[3]) == 0))
                    counts[kind] = counts.get(kind, 0) + 1
            self.sems = {}
            self.sizes = {}
            for kind, number in sorted(counts.items()):
                sem = agz_send if kind[0] == "Z" else agx_send
                self.sizes[kind] = friendly(number, 16 if kind[1] else 64)
                self.sems[kind] = [
                    sem.at[kind[1], at] for at, size in enumerate(self.sizes[kind]) for _ in range(size)
                ]
            self.sums = {}
            for act in program:
                if act[0] in ("RX", "FS"):
                    kind = self.link(*act)
                    self.sums[kind] = self.sums.get(kind, 0) + 1
            self.sums.pop("")
            for kind, number in sorted(self.sums.items()):
                sem = {"x": rsx_send, "z": rsz_send, "b": rsb_send}[kind]
                self.sizes[kind] = friendly(number, 16)
                self.sems[kind] = [sem.at[at] for at, size in enumerate(self.sizes[kind]) for _ in range(size)]
            self.slots = [[]]
            for act in program:
                if act[0] in ("GU", "GV", "DN"):
                    self.slots.append([])
                else:
                    self.slots[-1].append(act)
            self.order = [act[1:] for act in program if act[0] == "GU"]

        def toward(self, n):
            return device(slab[n], col, core)

        def run(self, at):
            for act in self.slots[at]:
                getattr(self, act[0])(*act[1:])

        def W(self, s, x, h):
            if not (s == self.near and x == 0):
                token_copy(s, x, h, agz_send.at[0, 0], beside).wait_recv()
            token_core(slab[s], column(x), h, True).start()

        def Z(self, s, x, h, n):
            token_copy(s, x, h, self.sems["Z", int(h == 0)].pop(), self.toward(n)).start()

        def X(self, s, h):
            token_copy(s, 0, h, self.sems["X", int(h == 0)].pop(), beside).start()

        def link(self, name, s, h, q):
            both = s != self.near and way_of(self.near, s, h, q) == 2
            if name == "RX":
                return "" if both else "x"
            return "" if s == self.near else "b" if both else "z"

        def RX(self, s, h, q):
            if not self.link("RX", s, h, q):
                return
            at = slab[s]
            part_core(at, h, q).wait_recv()
            total = core_sum(at, h, q, 1 - col)
            for n in range(ROWS):
                if s == self.near and n != s and way_of(n, s, h, q) == 2:
                    sum_both(at, h, q, slab[n], rsb_send.at[0], beside).wait_recv()
                    total = total + from_both[slab[n], at, h, q, 1 - col].astype(jnp.float32)
            to_x[at, h, q] = total.astype(jnp.bfloat16)
            sum_x(at, h, q, self.sems["x"].pop()).start()

        def FS(self, s, h, q):
            far = abs(self.near - s)
            at = slab[s]
            kind = self.link("FS", s, h, q)
            if kind == "b":
                part_core(at, h, q).wait_recv()
                total = core_sum(at, h, q, col)
                to_both[at, h, q, 1 - col] = core_sum(at, h, q, 1 - col).astype(jnp.bfloat16)
            else:
                sum_x(at, h, q, rsx_send.at[0]).wait_recv()
                total = core_sum(at, h, q, col) + from_x[at, h, q].astype(jnp.float32)
            for n in range(ROWS):
                how = way_of(n, s, h, q) if n != s else 0
                if far == 0 and how == 2:
                    total = total + from_both[slab[n], at, h, q, col].astype(jnp.float32)
                    continue
                beyond = abs(n - s) > far and (far == 0 or (n < self.near) == (self.near < s))
                if beyond and (how == 1 if far == 0 and abs(n - s) > 1 else how == 0 and abs(n - self.near) == 1):
                    sum_z(at, h, q, slab[n], rsz_send.at[0], beside).wait_recv()
                    total = total + from_z[slab[n], at, h, q].astype(jnp.float32)
            total = total.astype(jnp.bfloat16)
            if far == 0:
                out_ref[h * half : (h + 1) * half, q * cols : (q + 1) * cols] = total
                return
            n = self.near - 1 if s < self.near else self.near + 1
            if way_of(self.near, s, h, q):
                n = s
            if kind == "b":
                to_both[at, h, q, col] = total
                sum_both(at, h, q, row, self.sems["b"].pop(), self.toward(n)).start()
            else:
                to_z[at, h, q] = total
                sum_z(at, h, q, row, self.sems["z"].pop(), self.toward(n)).start()

        def sent(self):
            for kind, sizes in self.sizes.items():
                if kind in self.sums:
                    ref, sem = {"x": (to_x, rsx_send), "z": (to_z, rsz_send), "b": (to_both, rsb_send)}[kind]
                    for at, size in enumerate(sizes):
                        batch_sums(ref, size, sem.at[at]).wait()
                    continue
                name, h = kind
                sem = agz_send if name == "Z" else agx_send
                for at, size in enumerate(sizes):
                    batch(size, h, sem.at[h, at]).wait()

    lines = [(edge, Line(0, EDGE)), (jnp.logical_not(edge), Line(1, INNER))]

    def hook(at):
        for here, line in lines:
            if line.slots[at]:
                pl.when(here)(functools.partial(line.run, at))

    lane = lax.broadcasted_iota(jnp.int32, (4, GROUPS // HALVES, quarter, LANES), 3)
    group = lax.broadcasted_iota(jnp.int32, (4, GROUPS // HALVES, quarter, LANES), 1)

    def place(k):
        (s0, h0), (s1, h1) = lines[0][1].order[k], lines[1][1].order[k]
        s = slab[s0] if s0 == s1 else jnp.where(edge, slab[s0], slab[s1])
        return s, h0, h1

    at = 0
    for k in range(ROWS * HALVES):
        hook(at)
        s, h0, h1 = place(k)
        h = h0 if h0 == h1 else jnp.where(edge, h0, h1)
        if h0 == h1:
            for x in range(2):
                for g in range(GROUPS // HALVES):
                    token_core(s, x, h0 * (GROUPS // HALVES) + g, False).wait_recv()
        else:
            for (here, _), mine in zip(lines, (h0, h1)):
                @pl.when(here)
                def _():
                    for x in range(2):
                        for g in range(GROUPS // HALVES):
                            token_core(s, x, mine * (GROUPS // HALVES) + g, False).wait_recv()
        tables = tok[s, :, :, 0, :, width : width + LANES].reshape(4, 1, quarter, LANES).astype(jnp.float32)
        tables = jnp.broadcast_to(tables, (4, GROUPS // HALVES, quarter, LANES))
        pick = (lane // span == group + h * (GROUPS // HALVES)) & (lane % number == me)
        weight = jnp.sum(jnp.where(pick, tables, 0.0).reshape(4 * half, LANES), 1, keepdims=True)
        if k == 0:
            loads[0].wait()
            loads[1].wait()
        for j in range(PIECES):
            if j:
                hook(at)
            rows = tok[s, :, :, pl.ds(h * (GROUPS // HALVES), GROUPS // HALVES), :, 0:width].reshape(4 * half, width)
            here = slice(j * piece, (j + 1) * piece)
            gate_val = jnp.dot(rows, gate_w[:, here], preferred_element_type=jnp.float32)
            up_val = jnp.dot(rows, up_w[:, here], preferred_element_type=jnp.float32)
            hid[:, here] = (gate_val / (1.0 + jnp.exp(-gate_val)) * up_val).astype(jnp.bfloat16)
            at += 1
        if k == 0:
            loads[2].wait()
        for q in range(CHUNKS):
            hook(at)
            for b in range(0, cols, BLOCK):
                value = lax.dot_general(
                    hid[...], down_w[q * cols + b : q * cols + b + BLOCK, :], (((1,), (1,)), ((), ())),
                    preferred_element_type=jnp.float32,
                )
                part[s, h, q, :, :, :, b : b + BLOCK] = (
                    (value * weight).astype(jnp.bfloat16).reshape(2, 2, half, BLOCK)
                )
            part_core(s, h, q).start()
            at += 1
    hook(at)

    for here, line in lines:
        pl.when(here)(line.sent)
    batch(2 * ROWS, 1, agc_send.at[1]).wait()
    batch(2 * ROWS * (GROUPS - 1), 0, agc_send.at[0]).wait()
    pltpu.make_async_copy(from_core, from_core, other_send).wait()


def fused_body(tokens, expert_ids, router_weights, w_gate, w_up, w_down):
    count, width = tokens.shape
    ff = w_gate.shape[2]
    half = count // HALVES
    wide = width + LANES
    cols = width // CHUNKS
    bf16 = jnp.bfloat16
    dma = pltpu.SemaphoreType.DMA
    each = (ROWS, HALVES, CHUNKS)
    return pl.pallas_call(
        fused_kernel,
        out_shape=pltpu.VMEM((count, width), bf16),
        in_specs=[pl.BlockSpec(memory_space=pl.ANY)] * 6,
        out_specs=pl.BlockSpec(memory_space=pltpu.VMEM),
        scratch_shapes=[
            pltpu.VMEM((ROWS, 2, 2, GROUPS, count // GROUPS, wide), bf16),
            pltpu.VMEM(expert_ids.shape[::-1], jnp.int32),
            pltpu.VMEM(router_weights.shape[::-1], jnp.float32),
            pltpu.VMEM((width, ff), bf16),
            pltpu.VMEM((width, ff), bf16),
            pltpu.VMEM((width, ff), bf16),
            pltpu.VMEM((4 * half, ff), bf16),
            pltpu.VMEM(each + (2, 2, half, cols), bf16),
            pltpu.VMEM(each + (2, half, cols), bf16),
            pltpu.VMEM(each + (half, cols), bf16),
            pltpu.VMEM(each + (half, cols), bf16),
            pltpu.VMEM(each + (half, cols), bf16),
            pltpu.VMEM((ROWS,) + each + (half, cols), bf16),
            pltpu.VMEM(each + (2, half, cols), bf16),
            pltpu.VMEM((ROWS,) + each + (2, half, cols), bf16),
            dma((3,)), dma((3,)), dma((ROWS, 2, GROUPS)), dma((ROWS, 2, GROUPS)), dma(each), dma(each),
            dma((ROWS,) + each), dma((HALVES, 4)), dma((HALVES, 4)), dma((HALVES,)), dma,
            dma((4,)), dma((4,)), dma((4,)),
        ],
        compiler_params=pltpu.CompilerParams(
            collective_id=0, has_side_effects=True, vmem_limit_bytes=60 * 1024 * 1024
        ),
        name="moe",
    )(tokens.reshape(GROUPS, count // GROUPS, width), expert_ids.T, router_weights.T, w_gate, w_up, w_down)


def body(tokens, expert_ids, router_weights, w_gate, w_up, w_down):
    tok_count, top = expert_ids.shape
    experts = lax.axis_size("expert")
    cap = max(2, min(tok_count, 2 * tok_count * top // experts))
    args = (tokens, expert_ids, router_weights, w_gate, w_up, w_down)
    grid = experts == 4 * ROWS and lax.axis_size("dp") == 1 and tok_count % (16 * GROUPS) == 0 and TERMS * experts * GROUPS <= LANES
    grid = grid and w_gate.shape[2] % (PIECES * LANES) == 0 and tokens.shape[1] % (CHUNKS * BLOCK) == 0
    if cap >= tok_count and grid:
        return fused_body(*args)
    if cap >= tok_count:
        return dense_body(*args)
    return routed_body(cap, *args)


def solution(mesh):
    in_specs = (
        P(("parts", "expert", "dp"), None),
        P(("parts", "expert", "dp"), None),
        P(("parts", "expert", "dp"), None),
        P("expert", None, "dp"),
        P("expert", None, "dp"),
        P("expert", None, "dp"),
    )
    out_specs = P(("parts", "expert", "dp"), None)
    return jax.shard_map(body, mesh=mesh, in_specs=in_specs, out_specs=out_specs, check_vma=False)
```
